256 devices in a mesh: section: 16 (over x_lo, y, core), batch: 16 (over x_hi, z).
Axes of the slice: x: 4 (x_hi: 2, x_lo: 2; x = x_hi * 2 + x_lo), y: 4, z: 8, core: 2. Of those that a mesh axis runs over, the one named last changes fastest.
Arguments:
- states: bfloat16 [32, 32, 64, 1024], P('section', 'batch'), may hold values from -6 to 6
- weights: bfloat16 [32, 64, 576], P('section'), may hold values from -0.25 to 0.25
- guess: float32 [16, 32, 64, 1024], P('section', 'batch'), may hold values from -6 to 6
- loss_cotangent: float32 [32, 64, 1024], P('batch'), may hold values from -6 to 6
Outputs:
- start_cotangents: float32 [16, 32, 64, 1024], P('section', 'batch')
- weight_grads: float32 [32, 36864], P('section', 'batch')
The draws below stay inside these ranges and needn't reach their ends.
All inputs are finite; a program needn't handle non-finite values.
Results may differ from the reference program's by a relative error of at most 0.0039.
Values may be sent and summed in bfloat16 or wider, within the bound.
No kernel may reach another device: no remote copies, remote signals or barrier semaphores. Data moves between devices by JAX's collectives and lax.ppermute only.
A program may use at most 128 MiB of HBM per device.

```python
import math
import jax
import jax.numpy as jnp
from jax import lax

C = 64
SECTIONS = 16
LAYERS = 32
BATCH = 32
PIXELS = 1024


def block_scale(own_key, shape, cuts, least, top_value):
    level = 1.0
    for dim, shards_of in cuts:
        steps = jax.random.uniform(jax.random.fold_in(jax.random.fold_in(own_key, 6), dim), (shards_of,), jnp.float32, least / len(cuts), top_value / len(cuts))
        level = level * jnp.repeat(jnp.exp(steps), shape[dim] // shards_of).reshape((-1,) + (1,) * (len(shape) - 1 - dim))
    return level


def centred(own_key, extent, deviation, limit, shards=(), kind=jnp.bfloat16):
    values = deviation * jax.random.normal(own_key, extent, jnp.float32)
    if shards:
        values = values * block_scale(own_key, extent, shards, -0.22, 0.18)
    return jnp.clip(values, -limit, limit).astype(kind)


def setup_inputs(seed: int = 0) -> dict:
    arg_keys = jax.random.split(jax.random.key(seed), 5)
    return {
        "states": centred(arg_keys[0], (LAYERS, BATCH, C, PIXELS), 1.0, 6.0, ((0, 16), (1, 16))),
        "weights": centred(arg_keys[1], (LAYERS, C, 9 * C), (9 * C) ** -0.5, 0.25, ((0, 16),)),
        "guess": centred(arg_keys[2], (SECTIONS, BATCH, C, PIXELS), 1.0, 6.0, ((0, 16), (1, 16)), jnp.float32),
        "loss_cotangent": centred(arg_keys[3], (BATCH, C, PIXELS), 1.0, 6.0, ((0, 16),), jnp.float32),
    }


STEP = 0.0625

def unfold_taps(values, pixel_side, direction):
    length = values.shape[-1]
    margin = pixel_side + 1
    widths = [(0, 0)] * (values.ndim - 1) + [(margin, margin)]
    padded = jnp.pad(values, widths)
    column_base = jnp.arange(length) % pixel_side
    copies = []
    for row_step in (-1, 0, 1):
        for col_step in (-1, 0, 1):
            delta = direction * (row_step * pixel_side + col_step)
            window = lax.slice_in_dim(padded, margin + delta, margin + delta + length, axis=values.ndim - 1)
            column = column_base + direction * col_step
            inside = (column >= 0) & (column < pixel_side)
            copies.append(jnp.where(inside, window, jnp.zeros_like(window)))
    return jnp.stack(copies, axis=1)

def back_conv(weight, rounded, pixel_side):
    channels = weight.shape[0]
    kernel = weight.reshape(channels, 9, channels).astype(jnp.float32)
    stacked = unfold_taps(rounded, pixel_side, -1).astype(jnp.float32)
    return jnp.einsum('okc,bkop->bcp', kernel, stacked)

def advance(cotangent, rounded, layer_state, weight, step_size, pixel_side):
    activ = jnp.tanh(layer_state.astype(jnp.float32))
    return cotangent + step_size * (1.0 - activ * activ) * back_conv(weight, rounded, pixel_side)

def layer_grad(rounded, layer_state, pixel_side):
    activ = jnp.tanh(layer_state.astype(jnp.float32)).astype(jnp.bfloat16)
    stacked = unfold_taps(activ, pixel_side, 1).astype(jnp.float32)
    return (jnp.einsum('bop,bkcp->okc', rounded.astype(jnp.float32), stacked) * STEP).reshape(-1)

def reference(states, weights, guess, loss_cotangent):
    pixel_side = math.isqrt(states.shape[-1])
    sections = guess.shape[0]
    per_section = states.shape[0] // sections
    grouped_states = states.reshape((sections, per_section) + states.shape[1:])
    grouped_weights = weights.reshape((sections, per_section) + weights.shape[1:])

    def relax_section(packed):
        sec_states, sec_weights, initial = packed

        def fine_layer(cotangent, layer_pack):
            return (advance(cotangent, cotangent.astype(jnp.bfloat16), layer_pack[0], layer_pack[1], STEP, pixel_side), None)
        result, unused = lax.scan(fine_layer, initial, (sec_states, sec_weights), reverse=True)
        return result
    relaxed = lax.map(relax_section, (grouped_states, grouped_weights, guess))
    last_resid = (loss_cotangent - guess[-1])[None]
    residual = jnp.concatenate([relaxed[1:] - guess[:-1], last_resid], axis=0)

    def coarse_link(running, inputs):
        resid_row, first_state, first_weight = inputs
        value = advance(running, running.astype(jnp.bfloat16), first_state, first_weight, per_section * STEP, pixel_side) + resid_row
        return (value, value)
    unused, solved = lax.scan(coarse_link, residual[-1], (residual[:-1], grouped_states[1:, 0], grouped_weights[1:, 0]), reverse=True)
    correction = jnp.concatenate([solved, residual[-1:]], axis=0)
    new_guess = guess + correction

    def final_section(packed):
        sec_states, sec_weights, initial = packed

        def fine_layer(cotangent, layer_pack):
            layer_state, weight = layer_pack
            rounded = cotangent.astype(jnp.bfloat16)
            gradient = layer_grad(rounded, layer_state, pixel_side)
            return (advance(cotangent, rounded, layer_state, weight, STEP, pixel_side), gradient)
        result, gradients = lax.scan(fine_layer, initial, (sec_states, sec_weights), reverse=True)
        return (result, gradients)
    start_cot, gradients = lax.map(final_section, (grouped_states, grouped_weights, new_guess))
    return (start_cot, gradients.reshape(states.shape[0], -1))
```

```python
import functools

import jax
import jax.numpy as jnp
from jax import lax
from jax.experimental import pallas as pl
from jax.experimental.pallas import tpu as pltpu
from jax.sharding import PartitionSpec as P

H = 0.0625
SIDE = 32
C = 64
N = SIDE * SIDE
F32 = jnp.float32
BF16 = jnp.bfloat16
WIDE = 640
VMEM = pltpu.VMEM


def pixel(rows=C):
    return lax.broadcasted_iota(jnp.int32, (rows, N), 1)


def cols3(v):
    column = pixel() & (SIDE - 1)
    ahead = jnp.where(column < SIDE - 1, pltpu.roll(v, N - 1, 1), 0.0)
    behind = jnp.where(column > 0, pltpu.roll(v, 1, 1), 0.0)
    return jnp.concatenate([ahead.astype(BF16), v.astype(BF16), behind.astype(BF16)], axis=0)


def rows3(t):
    p = pixel()
    up = jnp.where(p >= SIDE, pltpu.roll(t, SIDE, 1), 0.0)
    down = jnp.where(p < N - SIDE, pltpu.roll(t, N - SIDE, 1), 0.0)
    return jnp.concatenate([up.astype(BF16), t.astype(BF16), down.astype(BF16)], axis=0)


def taps(w):
    blocks = [
        jnp.concatenate([w[:, (3 * a + b) * C : (3 * a + b + 1) * C] for a in range(3)], axis=1)
        for b in range(3)
    ]
    return jnp.concatenate(blocks, axis=0).astype(F32).T.astype(BF16)


def conv(m, x3):
    y = jnp.dot(m, x3, preferred_element_type=F32)
    p = pixel()
    low = jnp.where(p < N - SIDE, pltpu.roll(y[:C], N - SIDE, 1), 0.0)
    high = jnp.where(p >= SIDE, pltpu.roll(y[2 * C :], SIDE, 1), 0.0)
    return y[C : 2 * C] + low + high


def slope(u, scale):
    t = jnp.tanh(u.astype(F32))
    return scale - scale * (t * t)


def pack_kernel(states, weights, out):
    members = out.shape[0]
    m = taps(weights[0])
    for k in range(members):
        out[k, :, :N] = states[0, k % 2]
    flat = jnp.concatenate([m[a * C : (a + 1) * C] for a in range(3)], axis=1)
    for k in range(members):
        out[k, :, N : N + 9 * C] = flat


def source_kernel(states, weights, guess, loss, out):
    members = out.shape[0]
    m0, m1 = taps(weights[0]), taps(weights[1])
    for i in range(2):
        g = guess[0, i]
        t = slope(states[1, i], H) * conv(m1, cols3(g))
        v = t - g + 2.0 * loss[i]
        p = t + slope(states[0, i], H) * conv(m0, cols3(v))
        p = p.astype(BF16)
        for k in range(i, members, 2):
            out[k] = p


def chain_kernel(where, start, sources, packed, mine, other, last):
    members = sources.shape[0]

    def step(r, e):
        s = members - 1 - r

        @pl.when(s == where[0])
        def _():
            mine[...] = e

        @pl.when(s == where[1])
        def _():
            other[...] = e

        block = packed[s]
        flat = block[:, N : N + 9 * C]
        m = jnp.concatenate([flat[:, a * 3 * C : (a + 1) * 3 * C] for a in range(3)], axis=0)
        d = slope(block[:, :N], 2.0 * H)
        return e + sources[s].astype(F32) + d * conv(m, cols3(e))

    last[...] = lax.fori_loop(0, members, step, start[...])


def finish_kernel(which, states, weights, loss, mine, other, starts, grads):
    parts = grads.shape[0]
    rows = C // parts
    m0, m1 = taps(weights[0]), taps(weights[1])
    own = which[0]
    sums = [None, None]
    for i in range(2):
        e = jnp.where(own == i, mine[...], other[...])
        v = loss[i] + e
        for layer, m in ((1, m1), (0, m0)):
            t = jnp.tanh(states[layer, i].astype(F32))
            x3 = cols3(v)
            g = lax.dot_general(
                x3, rows3(t), (((1,), (1,)), ((), ())), preferred_element_type=F32
            )
            sums[layer] = g if i == 0 else sums[layer] + g
            v = v + (H - H * (t * t)) * conv(m, x3)
        starts[0, i] = v
    for layer in range(2):
        g = sums[layer] * H
        wide = jnp.concatenate(
            [g[b * C : (b + 1) * C, a * C : (a + 1) * C] for a in range(3) for b in range(3)], axis=1
        )
        for d in range(parts):
            grads[d, layer * rows : (layer + 1) * rows, :] = wide[d * rows : (d + 1) * rows]


def total_kernel(parts, out):
    rows = parts.shape[1] // 2
    s = parts[0]
    for d in range(1, parts.shape[0]):
        s = s + parts[d]
    for layer in range(2):
        out[layer : layer + 1, :] = jnp.concatenate(
            [s[layer * rows + r : layer * rows + r + 1] for r in range(rows)], axis=1
        )


def call(kernel, outs, n_scalar, n_in, flops, moved, name):
    smem = pl.BlockSpec(memory_space=pltpu.SMEM)
    vmem = pl.BlockSpec(memory_space=VMEM)
    return pl.pallas_call(
        kernel,
        out_shape=outs,
        in_specs=[smem] * n_scalar + [vmem] * n_in,
        out_specs=jax.tree.map(lambda _: vmem, outs),
        cost_estimate=pl.CostEstimate(flops=flops, bytes_accessed=moved, transcendentals=0),
        compiler_params=pltpu.CompilerParams(vmem_limit_bytes=40 << 20),
        name=name,
    )


def shards(states, weights, guess, loss):
    sections = lax.axis_size("section")
    nb = lax.axis_size("batch")
    members = sections // 2
    at = lax.axis_index("section")
    spot = lax.rem(at, members)
    core = lax.rem(at, 2)
    groups = [list(range(members)), list(range(members, sections))]
    shape = jax.ShapeDtypeStruct

    packed = call(pack_kernel, shape((members, C, N + WIDE), BF16), 0, 2, 10**6, 3 * 10**6, "pack")(states, weights)
    packed = lax.all_to_all(packed, "section", 0, 0, axis_index_groups=groups, tiled=True)
    sources = call(source_kernel, shape((members, C, N), BF16), 0, 4, 6 * 10**8, 3 * 10**6, "source")(
        states, weights, guess, loss
    )
    sources = lax.all_to_all(sources, "section", 0, 0, axis_index_groups=groups, tiled=True)

    image = shape((C, N), F32)
    where = jnp.stack([spot, spot ^ 1]).astype(jnp.int32)
    chain = call(chain_kernel, (image, image, image), 1, 3, 12 * 10**8, 4 * 10**6, "chain")
    zero = jnp.zeros((C, N), F32)
    last = chain(where, zero, sources, packed)[2]
    carried = lax.ppermute(last, "section", [(i, i - members) for i in range(members, sections)])
    mine, other, _ = chain(where, carried, sources, packed)
    other = lax.ppermute(other, "section", [(i, i ^ 1) for i in range(sections)])

    starts, grads = call(
        finish_kernel,
        (shape((1, 2, C, N), F32), shape((nb, 2 * (C // nb), 9 * C), F32)),
        1, 5, 12 * 10**8, 3 * 10**6, "finish",
    )(core.reshape(1).astype(jnp.int32), states, weights, loss, mine, other)
    grads = lax.all_to_all(grads, "batch", 0, 0, tiled=True)
    total = call(total_kernel, shape((2, 9 * C * C // nb), F32), 0, 1, 10**6, 10**6, "total")(grads)
    return starts, total


def solution(mesh):
    placed = (
        P("section", "batch", None, None),
        P("section", None, None),
        P("section", "batch", None, None),
        P("batch", None, None),
    )
    return jax.shard_map(
        shards,
        mesh=mesh,
        in_specs=placed,
        out_specs=(P("section", "batch", None, None), P("section", "batch")),
        check_vma=False,
    )
```

```python
import functools

import jax
import jax.numpy as jnp
from jax import lax
from jax.experimental import pallas as pl
from jax.experimental.pallas import tpu as pltpu
from jax.sharding import PartitionSpec as P

H = 0.0625
SIDE = 32
C = 64
N = SIDE * SIDE
F32 = jnp.float32
BF16 = jnp.bfloat16
WIDE = 640
WHOLE = 62 << 20
MOST = (63 << 20) + (1 << 18)


def pixel(rows=C):
    return lax.broadcasted_iota(jnp.int32, (rows, N), 1)


def cols3(v):
    column = pixel() & (SIDE - 1)
    ahead = jnp.where(column < SIDE - 1, pltpu.roll(v, N - 1, 1), 0.0)
    behind = jnp.where(column > 0, pltpu.roll(v, 1, 1), 0.0)
    return jnp.concatenate([ahead.astype(BF16), v.astype(BF16), behind.astype(BF16)], axis=0)


def rows3(t):
    p = pixel()
    up = jnp.where(p >= SIDE, pltpu.roll(t, SIDE, 1), 0.0)
    down = jnp.where(p < N - SIDE, pltpu.roll(t, N - SIDE, 1), 0.0)
    return jnp.concatenate([up.astype(BF16), t.astype(BF16), down.astype(BF16)], axis=0)


def taps(w):
    blocks = [
        jnp.concatenate([w[:, (3 * a + b) * C : (3 * a + b + 1) * C] for a in range(3)], axis=1)
        for b in range(3)
    ]
    return jnp.concatenate(blocks, axis=0).astype(F32).T.astype(BF16)


def conv(m, x3):
    y = jnp.dot(m, x3, preferred_element_type=F32)
    p = pixel()
    low = jnp.where(p < N - SIDE, pltpu.roll(y[:C], N - SIDE, 1), 0.0)
    high = jnp.where(p >= SIDE, pltpu.roll(y[2 * C :], SIDE, 1), 0.0)
    return y[C : 2 * C] + low + high


def slope(u, scale):
    t = jnp.tanh(u.astype(F32))
    return scale - scale * (t * t)


def moves(pairs, sems, first=0):
    made = [pltpu.make_async_copy(a, b, sems.at[first + n]) for n, (a, b) in enumerate(pairs)]
    for one in made:
        one.start()
    return made


def settle(made):
    for one in made:
        one.wait()


def source_kernel(states, weights, guess, loss, out, u, w, g, lc, p, flat, sems):
    members = out.shape[0]
    in_w, in_u, in_g, in_lc = moves([(weights, w), (states, u), (guess.at[0], g), (loss, lc)], sems)
    in_w.wait()
    m0, m1 = taps(w[0]), taps(w[1])
    zero = jnp.zeros((C, WIDE - 9 * C), BF16)
    flat[...] = jnp.concatenate([m0[a * C : (a + 1) * C] for a in range(3)] + [zero], axis=1)
    sent = moves([(flat, out.at[k, :, 2 * N :]) for k in range(members)], sems, 4)
    in_u.wait()
    sent += moves([(u.at[0, k % 2], out.at[k, :, :N]) for k in range(members)], sems, 4 + members)
    settle([in_g, in_lc])
    for i in range(2):
        t = slope(u[1, i], H) * conv(m1, cols3(g[i]))
        v = t - g[i] + 2.0 * lc[i]
        p[i] = (t + slope(u[0, i], H) * conv(m0, cols3(v))).astype(BF16)
        sent += moves(
            [(p.at[i], out.at[k, :, N : 2 * N]) for k in range(i, members, 2)],
            sems, 4 + 2 * members + i * (members // 2),
        )
    settle(sent)


def chain_kernel(where, start, packed, mine, other, last):
    members = packed.shape[0]

    def step(r, e):
        s = members - 1 - r

        @pl.when(s == where[0])
        def _():
            mine[...] = e

        @pl.when(s == where[1])
        def _():
            other[...] = e

        block = packed[s]
        flat = block[:, 2 * N : 2 * N + 9 * C]
        m = jnp.concatenate([flat[:, a * 3 * C : (a + 1) * 3 * C] for a in range(3)], axis=0)
        d = slope(block[:, :N], 2.0 * H)
        return e + block[:, N : 2 * N].astype(F32) + d * conv(m, cols3(e))

    last[...] = lax.fori_loop(0, members, step, start[...].astype(F32)).astype(BF16)


def finish_kernel(which, states, weights, loss, mine, other, starts, grads, u, w, lc, e, out, sems):
    parts = grads.shape[0]
    rows = C // parts
    own = which[0]
    in_w, *ins = moves(
        [(weights, w), (loss, lc), (states, u), (mine, e.at[own]), (other, e.at[1 - own])], sems
    )
    in_w.wait()
    m0, m1 = taps(w[0]), taps(w[1])
    settle(ins)
    sums = [None, None]
    sent = []
    for i in range(2):
        v = lc[i] + e[i]
        for layer, m in ((1, m1), (0, m0)):
            t = jnp.tanh(u[layer, i].astype(F32))
            x3 = cols3(v)
            g = lax.dot_general(
                x3, rows3(t), (((1,), (1,)), ((), ())), preferred_element_type=F32
            )
            sums[layer] = g if i == 0 else sums[layer] + g
            v = v + (H - H * (t * t)) * conv(m, x3)
        out[i] = v
        sent += moves([(out.at[i], starts.at[0, i])], sems, 5 + i)
    wides = []
    for layer in range(2):
        g = sums[layer] * H
        wides.append(jnp.concatenate(
            [g[b * C : (b + 1) * C, a * C : (a + 1) * C] for a in range(3) for b in range(3)], axis=1
        ))
    for d in range(parts):
        both = [wide[d * rows : (d + 1) * rows] for wide in wides]
        grads[d] = jnp.concatenate(both, axis=0).astype(grads.dtype)
    settle(sent)


def total_kernel(parts, out):
    rows = parts.shape[1] // 2
    s = parts[0].astype(F32)
    for d in range(1, parts.shape[0]):
        s = s + parts[d].astype(F32)
    for layer in range(2):
        out[layer : layer + 1, :] = jnp.concatenate(
            [s[layer * rows + r : layer * rows + r + 1] for r in range(rows)], axis=1
        )


def call(kernel, outs, where_in, where_out, scratch, n_sems, flops, moved, name, grant=32 << 20):
    spaces = {"s": pltpu.SMEM, "v": pltpu.VMEM, "h": pltpu.HBM}
    specs = lambda text: [pl.BlockSpec(memory_space=spaces[k]) for k in text]
    out_specs = specs(where_out)
    return pl.pallas_call(
        kernel,
        out_shape=outs,
        in_specs=specs(where_in),
        out_specs=tuple(out_specs) if isinstance(outs, tuple) else out_specs[0],
        scratch_shapes=[pltpu.VMEM(*one) for one in scratch]
        + ([pltpu.SemaphoreType.DMA((n_sems,))] if n_sems else []),
        cost_estimate=pl.CostEstimate(flops=flops, bytes_accessed=moved, transcendentals=0),
        compiler_params=pltpu.CompilerParams(vmem_limit_bytes=grant),
        name=name,
    )


def shards(states, weights, guess, loss):
    sections = lax.axis_size("section")
    nb = lax.axis_size("batch")
    members = sections // 2
    at = lax.axis_index("section")
    spot = lax.rem(at, members)
    core = lax.rem(at, 2)
    groups = [list(range(members)), list(range(members, sections))]
    shape = jax.ShapeDtypeStruct

    packed = call(
        source_kernel, shape((members, C, 2 * N + WIDE), BF16), "hhhh", "h",
        [((2, 2, C, N), BF16), ((2, C, 9 * C), BF16), ((2, C, N), F32), ((2, C, N), F32),
         ((2, C, N), BF16), ((C, WIDE), BF16)],
        4 + 3 * members, 6 * 10**8, 6 * 10**6, "source", WHOLE,
    )(states, weights, guess, loss)
    packed = lax.all_to_all(packed, "section", 0, 0, axis_index_groups=groups, tiled=True)

    image = shape((C, N), F32)
    where = jnp.stack([spot, spot ^ 1]).astype(jnp.int32)
    chain = call(
        chain_kernel, (image, image, shape((C, N), BF16)), "svv", "vvv", [], 0, 12 * 10**8, 4 * 10**6, "chain"
    )
    zero = jnp.zeros((C, N), BF16)
    last = chain(where, zero, packed)[2]
    carried = lax.ppermute(last, "section", [(i, i - members) for i in range(members, sections)])
    mine, other, _ = chain(where, carried, packed)
    other = lax.ppermute(other, "section", [(i, i ^ 1) for i in range(sections)])

    starts, grads = call(
        finish_kernel,
        (shape((1, 2, C, N), F32), shape((nb, 2 * (C // nb), 9 * C), BF16)),
        "shhhvv", "hv",
        [((2, 2, C, N), BF16), ((2, C, 9 * C), BF16), ((2, C, N), F32), ((2, C, N), F32), ((2, C, N), F32)],
        7, 12 * 10**8, 3 * 10**6, "finish", MOST,
    )(core.reshape(1).astype(jnp.int32), states, weights, loss, mine, other)
    grads = lax.all_to_all(grads, "batch", 0, 0, tiled=True)
    total = call(total_kernel, shape((2, 9 * C * C // nb), F32), "v", "v", [], 0, 10**6, 10**6, "total")(grads)
    return starts, total


def solution(mesh):
    placed = (
        P("section", "batch", None, None),
        P("section", None, None),
        P("section", "batch", None, None),
        P("batch", None, None),
    )
    return jax.shard_map(
        shards,
        mesh=mesh,
        in_specs=placed,
        out_specs=(P("section", "batch", None, None), P("section", "batch")),
        check_vma=False,
    )
```

```python
import jax
import jax.numpy as jnp
from jax import lax
from jax.experimental import pallas as pl
from jax.experimental.pallas import tpu as pltpu
from jax.sharding import PartitionSpec as P


H = 0.0625
SIDE = 32
C = 64
N = SIDE * SIDE
LANES = 128
F32 = jnp.float32
BF16 = jnp.bfloat16
WIDE = 640
WHOLE = 62 << 20


def masked(values, keep):
    return jnp.where(keep, values, jnp.zeros_like(values))


def lane(shape):
    return lax.broadcasted_iota(jnp.int32, shape, len(shape) - 1)


def cols3(v):
    v = v.astype(BF16)
    column = lane(v.shape) & (SIDE - 1)
    ahead = masked(pltpu.roll(v, N - 1, 1), column < SIDE - 1)
    behind = masked(pltpu.roll(v, 1, 1), column > 0)
    return jnp.concatenate([ahead, v, behind], axis=0)


def row_up(t):
    t = pltpu.roll(t, SIDE, 1)
    edge = t[:, :LANES]
    return jnp.concatenate([masked(edge, lane(edge.shape) >= SIDE), t[:, LANES:]], axis=1)


def row_down(t):
    t = pltpu.roll(t, N - SIDE, 1)
    edge = t[:, N - LANES :]
    return jnp.concatenate([t[:, : N - LANES], masked(edge, lane(edge.shape) < LANES - SIDE)], axis=1)


def rows3(t):
    t = t.astype(BF16)
    return jnp.concatenate([row_up(t), t, row_down(t)], axis=0)


def taps(w):
    blocks = [
        jnp.concatenate([w[:, (3 * a + b) * C : (3 * a + b + 1) * C] for a in range(3)], axis=1)
        for b in range(3)
    ]
    return jnp.concatenate(blocks, axis=0).astype(F32).T.astype(BF16)


def conv(m, x3):
    y = jnp.dot(m, x3, preferred_element_type=F32)
    low = row_down(y[:C].astype(BF16))
    high = row_up(y[2 * C :].astype(BF16))
    return y[C : 2 * C] + low.astype(F32) + high.astype(F32)


def flatten_taps(m):
    pad = jnp.zeros((C, WIDE - 9 * C), BF16)
    wide = [m[a * C : (a + 1) * C, : 2 * C] for a in range(3)]
    thin = [m[a * C : (a + 1) * C, 2 * C :] for a in range(3)]
    return jnp.concatenate(wide + thin + [pad], axis=1)


def unflatten_taps(flat):
    wide = [flat[:, 2 * C * a : 2 * C * (a + 1)] for a in range(3)]
    thin = [flat[:, (6 + a) * C : (7 + a) * C] for a in range(3)]
    return jnp.concatenate([jnp.concatenate(wide, axis=0), jnp.concatenate(thin, axis=0)], axis=1)


def moves(pairs, sems, first=0):
    made = [pltpu.make_async_copy(a, b, sems.at[first + n]) for n, (a, b) in enumerate(pairs)]
    for one in made:
        one.start()
    return made


def settle(made):
    for one in made:
        one.wait()


def source_kernel(states, weights, guess, loss, out, u, w, g, lc, send, flat, sems):
    members = out.shape[0]
    in_w, in_u, in_g, in_lc = moves([(weights, w), (states, u), (guess.at[0], g), (loss, lc)], sems)
    in_w.wait()
    m1, m0 = taps(w[1]), taps(w[0])
    flat[...] = flatten_taps(m0)
    sent = moves([(flat, out.at[k, :, 2 * N :]) for k in range(members)], sems, 4)
    settle([in_u, in_g, in_lc])
    for i in range(2):
        t1 = jnp.tanh(u[1, i].astype(F32))
        t0 = jnp.tanh(u[0, i].astype(F32))
        d0 = H - H * (t0 * t0)
        send[i, :, :N] = (2.0 * d0).astype(BF16)
        t = (H - H * (t1 * t1)) * conv(m1, cols3(g[i]))
        send[i, :, N:] = (t + d0 * conv(m0, cols3(t - g[i] + 2.0 * lc[i]))).astype(BF16)
        sent += moves(
            [(send.at[i], out.at[k, :, : 2 * N]) for k in range(i, members, 2)],
            sems, 4 + members + i * (members // 2),
        )
    settle(sent)


def prep_kernel(which, states, weights, loss, ms, acts, slopes, base):
    base[...] = loss[which[0]]
    for layer in range(2):
        ms[layer] = taps(weights[layer])
        for i in range(2):
            t = jnp.tanh(states[layer, i].astype(F32))
            acts[layer, i] = rows3(t)
            slopes[layer, i] = H - H * (t * t)


def chain_kernel(where, start, packed, base, mine, other, last):
    members = packed.shape[0]

    def step(r, e):
        s = members - 1 - r

        @pl.when(s == where[0])
        def _():
            mine[...] = e + base[...]

        @pl.when(s == where[1])
        def _():
            other[...] = e + base[...]

        m = unflatten_taps(packed[s, :, 2 * N :])
        y = conv(m, cols3(e))
        return e + packed[s, :, N : 2 * N].astype(F32) + packed[s, :, :N].astype(F32) * y

    last[...] = lax.fori_loop(0, members, step, start[...].astype(F32)).astype(BF16)


def finish_kernel(which, ms, acts, slopes, mine, other, grads, x3s, lams):
    parts = grads.shape[0]
    rows = C // parts
    own = which[0]
    sums = [None, None]
    for i in range(2):
        v = jnp.where(own == i, mine[...], other[...])
        for layer in (1, 0):
            x3 = cols3(v)
            g = lax.dot_general(
                x3, acts[layer, i], (((1,), (1,)), ((), ())), preferred_element_type=F32
            )
            sums[layer] = g if i == 0 else sums[layer] + g
            if layer:
                v = v + slopes[layer, i] * conv(ms[layer], x3)
        x3s[i] = x3
        lams[i] = v
    wides = []
    for layer in range(2):
        g = sums[layer] * H
        wides.append(jnp.concatenate(
            [g[b * C : (b + 1) * C, a * C : (a + 1) * C] for a in range(3) for b in range(3)], axis=1
        ))
    for d in range(parts):
        both = [wide[d * rows : (d + 1) * rows] for wide in wides]
        grads[d] = jnp.concatenate(both, axis=0).astype(grads.dtype)


def start_kernel(ms, slopes, x3s, lams, starts):
    for i in range(2):
        starts[0, i] = lams[i] + slopes[0, i] * conv(ms[0], x3s[i])


def total_kernel(parts, out):
    rows = parts.shape[1] // 2
    s = parts[0].astype(F32)
    for d in range(1, parts.shape[0]):
        s = s + parts[d].astype(F32)
    for layer in range(2):
        out[layer : layer + 1, :] = jnp.concatenate(
            [s[layer * rows + r : layer * rows + r + 1] for r in range(rows)], axis=1
        )


def call(kernel, outs, where_in, where_out, scratch, n_sems, flops, moved, grant=16 << 20):
    spaces = {"s": pltpu.SMEM, "v": pltpu.VMEM, "h": pltpu.HBM}
    specs = lambda text: [pl.BlockSpec(memory_space=spaces[k]) for k in text]
    out_specs = specs(where_out)
    return pl.pallas_call(
        kernel,
        out_shape=outs,
        in_specs=specs(where_in),
        out_specs=tuple(out_specs) if isinstance(outs, tuple) else out_specs[0],
        scratch_shapes=[pltpu.VMEM(*one) for one in scratch]
        + ([pltpu.SemaphoreType.DMA((n_sems,))] if n_sems else []),
        cost_estimate=pl.CostEstimate(flops=flops, bytes_accessed=moved, transcendentals=0),
        compiler_params=pltpu.CompilerParams(vmem_limit_bytes=grant),
    )


def shards(states, weights, guess, loss):
    sections = lax.axis_size("section")
    nb = lax.axis_size("batch")
    members = sections // 2
    at = lax.axis_index("section")
    spot = lax.rem(at, members)
    core = lax.rem(at, 2)
    groups = [list(range(members)), list(range(members, sections))]
    shape = jax.ShapeDtypeStruct
    image = shape((C, N), F32)
    which = core.reshape(1).astype(jnp.int32)

    source = call(
        source_kernel, shape((members, C, 2 * N + WIDE), BF16), "hhhh", "h",
        [((2, 2, C, N), BF16), ((2, C, 9 * C), BF16), ((2, C, N), F32), ((2, C, N), F32),
         ((2, C, 2 * N), BF16), ((C, WIDE), BF16)],
        4 + 2 * members, 6 * 10**8, 6 * 10**6, WHOLE,
    )(states, weights, guess, loss)
    packed = lax.all_to_all(source, "section", 0, 0, axis_index_groups=groups, tiled=True)
    ms, acts, slopes, base = call(
        prep_kernel,
        (shape((2, 3 * C, 3 * C), BF16), shape((2, 2, 3 * C, N), BF16), shape((2, 2, C, N), F32), image),
        "svvv", "vvvv", [], 0, 10**8, 4 * 10**6,
    )(which, states, weights, loss)

    where = jnp.stack([spot, spot ^ 1]).astype(jnp.int32)
    chain = call(chain_kernel, (image, image, shape((C, N), BF16)), "svvv", "vvv", [], 0, 12 * 10**8, 4 * 10**6)
    zero = jnp.zeros((C, N), BF16)
    last = chain(where, zero, packed, base)[2]
    carried = lax.ppermute(last, "section", [(i, i - members) for i in range(members, sections)])
    mine, other, _ = chain(where, carried, packed, base)
    other = lax.ppermute(other, "section", [(i, i ^ 1) for i in range(sections)])

    grads, x3s, lams = call(
        finish_kernel,
        (shape((nb, 2 * (C // nb), 9 * C), BF16), shape((2, 3 * C, N), BF16), shape((2, C, N), F32)),
        "svvvvv", "vvv", [], 0, 12 * 10**8, 3 * 10**6,
    )(which, ms, acts, slopes, mine, other)
    grads = lax.all_to_all(grads, "batch", 0, 0, tiled=True)
    starts = call(start_kernel, shape((1, 2, C, N), F32), "vvvv", "v", [], 0, 3 * 10**8, 3 * 10**6)(
        ms, slopes, x3s, lams
    )
    total = call(total_kernel, shape((2, 9 * C * C // nb), F32), "v", "v", [], 0, 10**6, 10**6)(grads)
    return starts, total


def solution(mesh):
    placed = (
        P("section", "batch", None, None),
        P("section", None, None),
        P("section", "batch", None, None),
        P("batch", None, None),
    )
    return jax.shard_map(
        shards,
        mesh=mesh,
        in_specs=placed,
        out_specs=(P("section", "batch", None, None), P("section", "batch")),
        check_vma=False,
    )
```

```python
import jax
import jax.numpy as jnp
from jax import lax
from jax.experimental import pallas as pl
from jax.experimental.pallas import tpu as pltpu
from jax.sharding import PartitionSpec as P


H = 0.0625
SIDE = 32
C = 64
N = SIDE * SIDE
LANES = 128
F32 = jnp.float32
BF16 = jnp.bfloat16
WIDE = 640
WHOLE = 62 << 20


def masked(values, keep):
    return jnp.where(keep, values, jnp.zeros_like(values))


def lane(shape):
    return lax.broadcasted_iota(jnp.int32, shape, len(shape) - 1)


def cols3(v):
    v = v.astype(BF16)
    column = lane(v.shape) & (SIDE - 1)
    ahead = masked(pltpu.roll(v, N - 1, 1), column < SIDE - 1)
    behind = masked(pltpu.roll(v, 1, 1), column > 0)
    return jnp.concatenate([ahead, v, behind], axis=0)


def row_up(t):
    t = pltpu.roll(t, SIDE, 1)
    edge = t[:, :LANES]
    return jnp.concatenate([masked(edge, lane(edge.shape) >= SIDE), t[:, LANES:]], axis=1)


def row_down(t):
    t = pltpu.roll(t, N - SIDE, 1)
    edge = t[:, N - LANES :]
    return jnp.concatenate([t[:, : N - LANES], masked(edge, lane(edge.shape) < LANES - SIDE)], axis=1)


def rows3(t):
    t = t.astype(BF16)
    return jnp.concatenate([row_up(t), t, row_down(t)], axis=0)


def taps(w):
    blocks = [
        jnp.concatenate([w[:, (3 * a + b) * C : (3 * a + b + 1) * C] for a in range(3)], axis=1)
        for b in range(3)
    ]
    return jnp.concatenate(blocks, axis=0).astype(F32).T.astype(BF16)


def conv(m, x3):
    y = jnp.dot(m, x3, preferred_element_type=F32)
    low = row_down(y[:C].astype(BF16))
    high = row_up(y[2 * C :].astype(BF16))
    return y[C : 2 * C] + low.astype(F32) + high.astype(F32)


def flatten_taps(m):
    pad = jnp.zeros((C, WIDE - 9 * C), BF16)
    wide = [m[a * C : (a + 1) * C, : 2 * C] for a in range(3)]
    thin = [m[a * C : (a + 1) * C, 2 * C :] for a in range(3)]
    return jnp.concatenate(wide + thin + [pad], axis=1)


def unflatten_taps(flat):
    wide = [flat[:, 2 * C * a : 2 * C * (a + 1)] for a in range(3)]
    thin = [flat[:, (6 + a) * C : (7 + a) * C] for a in range(3)]
    return jnp.concatenate([jnp.concatenate(wide, axis=0), jnp.concatenate(thin, axis=0)], axis=1)


def moves(pairs, sems, first=0):
    made = [pltpu.make_async_copy(a, b, sems.at[first + n]) for n, (a, b) in enumerate(pairs)]
    for one in made:
        one.start()
    return made


def settle(made):
    for one in made:
        one.wait()


def part_of(u, g, lc, m0, m1):
    t1 = jnp.tanh(u[1].astype(F32))
    t0 = jnp.tanh(u[0].astype(F32))
    d0 = H - H * (t0 * t0)
    t = (H - H * (t1 * t1)) * conv(m1, cols3(g))
    p = t + d0 * conv(m0, cols3(t - g + 2.0 * lc))
    return (2.0 * d0).astype(BF16), p.astype(BF16)


def give_kernel(which, states, weights, guess, loss, out, ms, u, w, g, lc, sems):
    i = 1 - which[0]
    in_w, *ins = moves(
        [(weights, w), (states.at[1, i], u.at[1]), (states.at[0, i], u.at[0]), (guess.at[0, i], g), (loss.at[i], lc)],
        sems,
    )
    in_w.wait()
    m1, m0 = taps(w[1]), taps(w[0])
    ms[0], ms[1] = m0, m1
    out[:, 2 * N :] = flatten_taps(m0)
    settle(ins)
    out[:, :N], out[:, N : 2 * N] = part_of(u, g[...], lc[...], m0, m1)


def keep_kernel(which, states, guess, loss, ms, out, u, g, lc, sems):
    i = which[0]
    settle(moves(
        [(states.at[1, i], u.at[1]), (states.at[0, i], u.at[0]), (guess.at[0, i], g), (loss.at[i], lc)], sems
    ))
    out[:, :N], out[:, N:] = part_of(u, g[...], lc[...], ms[0], ms[1])


def merge_kernel(which, keep, got, ms, out, odd, pair, sems):
    even = which[0] == 0
    mine, theirs = flatten_taps(ms[0]), got[:, 2 * N :]
    p_even = jnp.where(even, keep[:, N:], got[:, N : 2 * N])
    p_odd = jnp.where(even, got[:, N : 2 * N], keep[:, N:])
    d_even = jnp.where(even, keep[:, :N], got[:, :N])
    taps_even = jnp.where(even, mine, theirs)
    pair[:, :N] = d_even
    pair[:, N : 2 * N] = jnp.where(even, got[:, :N], keep[:, :N])
    pair[:, 3 * N : 3 * N + WIDE] = taps_even
    pair[:, 3 * N + WIDE :] = jnp.where(even, theirs, mine)
    odd[...] = p_odd
    y = conv(unflatten_taps(taps_even), cols3(p_odd))
    merged = p_even.astype(F32) + p_odd.astype(F32) + d_even.astype(F32) * y
    pair[:, 2 * N : 3 * N] = merged.astype(BF16)
    settle(moves([(pair, out.at[k]) for k in range(out.shape[0])], sems))


def prep_kernel(which, states, loss, acts, slopes, base):
    base[...] = loss[which[0]]
    for layer in range(2):
        for i in range(2):
            t = jnp.tanh(states[layer, i].astype(F32))
            acts[layer, i] = rows3(t)
            slopes[layer, i] = H - H * (t * t)


def apply(packed, k, which, e):
    m = unflatten_taps(packed[k, :, 3 * N + which * WIDE : 3 * N + (which + 1) * WIDE])
    return e + packed[k, :, which * N : (which + 1) * N].astype(F32) * conv(m, cols3(e))


def upper_kernel(packed, last):
    chips = packed.shape[0]

    def step(r, e):
        k = chips - 1 - r
        x = apply(packed, k, 1, e)
        return apply(packed, k, 0, x) + packed[k, :, 2 * N : 3 * N].astype(F32)

    e = packed[chips - 1, :, 2 * N : 3 * N].astype(F32)
    last[...] = lax.fori_loop(1, chips, step, e).astype(BF16)


def lower_kernel(where, which, start, packed, odd, base, mine, other, high, low):
    chips = packed.shape[0]

    def step(r, e):
        k = chips - 1 - r
        x = apply(packed, k, 1, e)

        @pl.when(k == where[0])
        def _():
            high[...] = e
            low[...] = x

        return apply(packed, k, 0, x) + packed[k, :, 2 * N : 3 * N].astype(F32)

    lax.fori_loop(0, chips, step, start[...].astype(F32))
    at_high = high[...] + base[...]
    at_low = low[...] + odd[...].astype(F32) + base[...]
    even = which[0] == 0
    mine[...] = jnp.where(even, at_low, at_high)
    other[...] = jnp.where(even, at_high, at_low)


def finish(i, ms, acts, slopes, v, x3_out, lam_out):
    x3 = cols3(v)
    products = [None, lax.dot_general(x3, acts[1, i], (((1,), (1,)), ((), ())), preferred_element_type=F32)]
    v = v + slopes[1, i] * conv(ms[1], x3)
    x3 = cols3(v)
    products[0] = lax.dot_general(x3, acts[0, i], (((1,), (1,)), ((), ())), preferred_element_type=F32)
    x3_out[...] = x3
    lam_out[...] = v
    return products


def own_kernel(which, ms, acts, slopes, mine, sums, x3, lam):
    sums[0], sums[1] = finish(which[0], ms, acts, slopes, mine[...], x3, lam)


def other_kernel(which, ms, acts, slopes, other, sums, grads, x3, lam):
    products = finish(1 - which[0], ms, acts, slopes, other[...], x3, lam)
    near, far = grads.shape[:2]
    rows = C // (near * far)
    wides = []
    for layer in range(2):
        g = (sums[layer] + products[layer]) * H
        wides.append(jnp.concatenate(
            [g[b * C : (b + 1) * C, a * C : (a + 1) * C] for a in range(3) for b in range(3)], axis=1
        ))
    for d in range(near * far):
        both = [wide[d * rows : (d + 1) * rows] for wide in wides]
        grads[d % near, d // near] = jnp.concatenate(both, axis=0).astype(grads.dtype)


def start_kernel(which, ms, slopes, x3_own, lam_own, x3_other, lam_other, starts):
    for i, x3, lam in ((which[0], x3_own, lam_own), (1 - which[0], x3_other, lam_other)):
        starts[0, i] = lam[...] + slopes[0, i] * conv(ms[0], x3[...])


def sum_kernel(parts, out):
    s = parts[0].astype(F32)
    for d in range(1, parts.shape[0]):
        s = s + parts[d].astype(F32)
    out[...] = s


def total_kernel(parts, out):
    rows = parts.shape[1] // 2
    s = parts[0].astype(F32)
    for d in range(1, parts.shape[0]):
        s = s + parts[d].astype(F32)
    for layer in range(2):
        out[layer : layer + 1, :] = jnp.concatenate(
            [s[layer * rows + r : layer * rows + r + 1] for r in range(rows)], axis=1
        )


def call(kernel, outs, where_in, where_out, scratch, n_sems, flops, moved, grant=16 << 20):
    spaces = {"s": pltpu.SMEM, "v": pltpu.VMEM, "h": pltpu.HBM}
    specs = lambda text: [pl.BlockSpec(memory_space=spaces[k]) for k in text]
    out_specs = specs(where_out)
    return pl.pallas_call(
        kernel,
        out_shape=outs,
        in_specs=specs(where_in),
        out_specs=tuple(out_specs) if isinstance(outs, tuple) else out_specs[0],
        scratch_shapes=[pltpu.VMEM(*one) for one in scratch]
        + ([pltpu.SemaphoreType.DMA((n_sems,))] if n_sems else []),
        cost_estimate=pl.CostEstimate(flops=flops, bytes_accessed=moved, transcendentals=0),
        compiler_params=pltpu.CompilerParams(vmem_limit_bytes=grant),
    )


def reduce_scatter(grads):
    near, far = grads.shape[:2]
    shape = jax.ShapeDtypeStruct
    quads = [[q * near + n for n in range(near)] for q in range(far)]
    parts = lax.all_to_all(grads, "batch", 0, 0, axis_index_groups=quads, tiled=True)
    summed = call(sum_kernel, shape(grads.shape[1:], F32), "v", "v", [], 0, 10**6, 10**6)(parts)
    if far > 1:
        across = [[q * near + n for q in range(far)] for n in range(near)]
        summed = lax.all_to_all(summed, "batch", 0, 0, axis_index_groups=across, tiled=True)
    rows, columns = grads.shape[2:]
    return call(total_kernel, shape((2, rows // 2 * columns), F32), "v", "v", [], 0, 10**6, 10**6)(summed)


def shards(states, weights, guess, loss):
    sections = lax.axis_size("section")
    nb = lax.axis_size("batch")
    half = sections // 2
    chips = half // 2
    at = lax.axis_index("section")
    spot = (lax.rem(at, half) // 2).reshape(1).astype(jnp.int32)
    which = lax.rem(at, 2).reshape(1).astype(jnp.int32)
    shape = jax.ShapeDtypeStruct
    image, image16 = shape((C, N), F32), shape((C, N), BF16)
    near = min(4, nb)

    swap = [(i, i ^ 1) for i in range(sections)]
    give, ms = call(
        give_kernel, (shape((C, 2 * N + WIDE), BF16), shape((2, 3 * C, 3 * C), BF16)), "shhhh", "vv",
        [((2, C, N), BF16), ((2, C, 9 * C), BF16), ((C, N), F32), ((C, N), F32)],
        5, 3 * 10**8, 2 * 10**6, WHOLE,
    )(which, states, weights, guess, loss)
    got = lax.ppermute(give, "section", swap)
    keep = call(
        keep_kernel, shape((C, 2 * N), BF16), "shhhv", "v",
        [((2, C, N), BF16), ((C, N), F32), ((C, N), F32)], 4, 3 * 10**8, 2 * 10**6, WHOLE,
    )(which, states, guess, loss, ms)
    pairs, odd = call(
        merge_kernel, (shape((chips, C, 3 * N + 2 * WIDE), BF16), image16), "svvv", "hv",
        [((C, 3 * N + 2 * WIDE), BF16)], chips, 10**8, 3 * 10**6,
    )(which, keep, got, ms)
    groups = [[x * half + 2 * y + c for y in range(chips)] for x in range(2) for c in range(2)]
    packed = lax.all_to_all(pairs, "section", 0, 0, axis_index_groups=groups, tiled=True)
    acts, slopes, base = call(
        prep_kernel, (shape((2, 2, 3 * C, N), BF16), shape((2, 2, C, N), F32), image),
        "svv", "vvv", [], 0, 10**8, 4 * 10**6,
    )(which, states, loss)

    last = call(upper_kernel, image16, "v", "v", [], 0, 10**9, 2 * 10**6)(packed)
    carried = lax.ppermute(last, "section", [(i, i - half) for i in range(half, sections)])
    mine, other = call(
        lower_kernel, (image, image), "ssvvvv", "vv", [((C, N), F32), ((C, N), F32)], 0, 12 * 10**8, 2 * 10**6
    )(spot, which, carried, packed, odd, base)
    theirs = lax.ppermute(other, "section", swap)

    x3_shape = shape((3 * C, N), BF16)
    sums, x3_own, lam_own = call(
        own_kernel, (shape((2, 3 * C, 3 * C), F32), x3_shape, image), "svvvv", "vvv", [], 0, 4 * 10**8, 10**6
    )(which, ms, acts, slopes, mine)
    grads, x3_other, lam_other = call(
        other_kernel, (shape((near, nb // near, 2 * (C // nb), 9 * C), BF16), x3_shape, image),
        "svvvvv", "vvv", [], 0, 4 * 10**8, 10**6,
    )(which, ms, acts, slopes, theirs, sums)
    starts = call(start_kernel, shape((1, 2, C, N), F32), "svvvvvv", "v", [], 0, 3 * 10**8, 3 * 10**6)(
        which, ms, slopes, x3_own, lam_own, x3_other, lam_other
    )
    return starts, reduce_scatter(grads)


def solution(mesh):
    placed = (
        P("section", "batch", None, None),
        P("section", None, None),
        P("section", "batch", None, None),
        P("batch", None, None),
    )
    return jax.shard_map(
        shards,
        mesh=mesh,
        in_specs=placed,
        out_specs=(P("section", "batch", None, None), P("section", "batch")),
        check_vma=False,
    )
```

```python
import jax
import jax.numpy as jnp
from jax import lax
from jax.experimental import pallas as pl
from jax.experimental.pallas import tpu as pltpu
from jax.sharding import PartitionSpec as P


H = 0.0625
SIDE = 32
C = 64
N = SIDE * SIDE
LANES = 128
F32 = jnp.float32
BF16 = jnp.bfloat16
WIDE = 640
LEAD = 2 * N + 2 * WIDE
WHOLE = 62 << 20


def masked(values, keep):
    return jnp.where(keep, values, jnp.zeros_like(values))


def lane(shape):
    return lax.broadcasted_iota(jnp.int32, shape, len(shape) - 1)


def cols3(v):
    v = v.astype(BF16)
    column = lane(v.shape) & (SIDE - 1)
    ahead = masked(pltpu.roll(v, N - 1, 1), column < SIDE - 1)
    behind = masked(pltpu.roll(v, 1, 1), column > 0)
    return jnp.concatenate([ahead, v, behind], axis=0)


def row_up(t):
    t = pltpu.roll(t, SIDE, 1)
    edge = t[:, :LANES]
    return jnp.concatenate([masked(edge, lane(edge.shape) >= SIDE), t[:, LANES:]], axis=1)


def row_down(t):
    t = pltpu.roll(t, N - SIDE, 1)
    edge = t[:, N - LANES :]
    return jnp.concatenate([t[:, : N - LANES], masked(edge, lane(edge.shape) < LANES - SIDE)], axis=1)


def rows3(t):
    t = t.astype(BF16)
    return jnp.concatenate([row_up(t), t, row_down(t)], axis=0)


def taps(w):
    blocks = [
        jnp.concatenate([w[:, (3 * a + b) * C : (3 * a + b + 1) * C] for a in range(3)], axis=1)
        for b in range(3)
    ]
    return jnp.concatenate(blocks, axis=0).astype(F32).T.astype(BF16)


def conv(m, x3):
    y = jnp.dot(m, x3, preferred_element_type=F32)
    low = row_down(y[:C].astype(BF16))
    high = row_up(y[2 * C :].astype(BF16))
    return y[C : 2 * C] + low.astype(F32) + high.astype(F32)


def flatten_taps(m):
    pad = jnp.zeros((C, WIDE - 9 * C), BF16)
    wide = [m[a * C : (a + 1) * C, : 2 * C] for a in range(3)]
    thin = [m[a * C : (a + 1) * C, 2 * C :] for a in range(3)]
    return jnp.concatenate(wide + thin + [pad], axis=1)


def unflatten_taps(flat):
    wide = [flat[:, 2 * C * a : 2 * C * (a + 1)] for a in range(3)]
    thin = [flat[:, (6 + a) * C : (7 + a) * C] for a in range(3)]
    return jnp.concatenate([jnp.concatenate(wide, axis=0), jnp.concatenate(thin, axis=0)], axis=1)


def core():
    return lax.rem(lax.axis_index("section"), 2)


def moves(pairs, sems, first=0):
    made = [pltpu.make_async_copy(a, b, sems.at[first + n]) for n, (a, b) in enumerate(pairs)]
    for one in made:
        one.start()
    return made


def settle(made):
    for one in made:
        one.wait()


def part_of(u, g, lc, m0, m1):
    t1 = jnp.tanh(u[1].astype(F32))
    t0 = jnp.tanh(u[0].astype(F32))
    d0 = H - H * (t0 * t0)
    t = (H - H * (t1 * t1)) * conv(m1, cols3(g))
    p = t + d0 * conv(m0, cols3(t - g + 2.0 * lc))
    return (2.0 * d0).astype(BF16), p.astype(BF16)


def source_kernel(states, weights, guess, loss, give, keep, ms, u, w, g, lc, sems):
    own = core()
    in_w, *ins = moves([(weights, w), (states, u), (guess.at[0], g), (loss, lc)], sems)
    in_w.wait()
    m1, m0 = taps(w[1]), taps(w[0])
    ms[0], ms[1] = m0, m1
    give[:, 2 * N :] = flatten_taps(m0)
    settle(ins)
    for i, out in ((1 - own, give), (own, keep)):
        out[:, :N], out[:, N : 2 * N] = part_of(u.at[:, i], g[i], lc[i], m0, m1)


def merge_kernel(keep, got, ms, out, odd, pair, sems):
    even = core() == 0
    mine, theirs = flatten_taps(ms[0]), got[:, 2 * N :]
    d_even = jnp.where(even, keep[:, :N], got[:, :N])
    taps_even = jnp.where(even, mine, theirs)
    pair[:, :N] = d_even
    pair[:, N : 2 * N] = jnp.where(even, got[:, :N], keep[:, :N])
    pair[:, 2 * N : 2 * N + WIDE] = taps_even
    pair[:, 2 * N + WIDE : LEAD] = jnp.where(even, theirs, mine)
    chips = out.shape[0]
    sent = moves([(pair.at[:, :LEAD], out.at[k, :, :LEAD]) for k in range(chips)], sems)
    p_even = jnp.where(even, keep[:, N:], got[:, N : 2 * N])
    p_odd = jnp.where(even, got[:, N : 2 * N], keep[:, N:])
    odd[...] = p_odd
    y = conv(unflatten_taps(taps_even), cols3(p_odd))
    merged = p_even.astype(F32) + p_odd.astype(F32) + d_even.astype(F32) * y
    pair[:, LEAD:] = merged.astype(BF16)
    settle(sent + moves([(pair.at[:, LEAD:], out.at[k, :, LEAD:]) for k in range(chips)], sems, chips))


def prep_kernel(states, loss, acts, slopes, base):
    base[...] = loss[core()]
    for layer in range(2):
        for i in range(2):
            t = jnp.tanh(states[layer, i].astype(F32))
            acts[layer, i] = rows3(t)
            slopes[layer, i] = H - H * (t * t)


def apply(packed, k, which, e):
    m = unflatten_taps(packed[k, :, 2 * N + which * WIDE : 2 * N + (which + 1) * WIDE])
    return e + packed[k, :, which * N : (which + 1) * N].astype(F32) * conv(m, cols3(e))


def arrivals(source, packed, sems):
    made = [pltpu.make_async_copy(source.at[k], packed.at[k], sems.at[k]) for k in range(packed.shape[0])]
    for one in made[::-1]:
        one.start()
    return lambda k: pltpu.make_async_copy(source.at[k], packed.at[k], sems.at[k]).wait()


def upper_kernel(source, last, packed, sems):
    chips = packed.shape[0]
    arrived = arrivals(source, packed, sems)

    def step(r, e):
        k = chips - 1 - r
        arrived(k)
        x = apply(packed, k, 1, e)
        return apply(packed, k, 0, x) + packed[k, :, LEAD:].astype(F32)

    arrived(chips - 1)
    e = packed[chips - 1, :, LEAD:].astype(F32)
    last[...] = lax.fori_loop(1, chips, step, e).astype(BF16)


def lower_kernel(start, source, odd, base, mine, other, high, low, packed, sems):
    chips = packed.shape[0]
    arrived = arrivals(source, packed, sems)

    def step(r, e):
        k = chips - 1 - r
        arrived(k)
        x = apply(packed, k, 1, e)

        @pl.when(k == lax.rem(lax.axis_index("section") // 2, chips))
        def _():
            high[...] = e
            low[...] = x

        return apply(packed, k, 0, x) + packed[k, :, LEAD:].astype(F32)

    lax.fori_loop(0, chips, step, start[...].astype(F32))
    at_high = high[...] + base[...]
    at_low = low[...] + odd[...].astype(F32) + base[...]
    even = core() == 0
    mine[...] = jnp.where(even, at_low, at_high)
    other[...] = jnp.where(even, at_high, at_low)


def finish(i, ms, acts, slopes, v):
    x3 = cols3(v)
    first = lax.dot_general(x3, acts[1, i], (((1,), (1,)), ((), ())), preferred_element_type=F32)
    x3 = cols3(v + slopes[1, i] * conv(ms[1], x3))
    return lax.dot_general(x3, acts[0, i], (((1,), (1,)), ((), ())), preferred_element_type=F32), first


def own_kernel(ms, acts, slopes, mine, sums):
    sums[0], sums[1] = finish(core(), ms, acts, slopes, mine[...])


def other_kernel(ms, acts, slopes, other, sums, grads):
    products = finish(1 - core(), ms, acts, slopes, other[...])
    parts = grads.shape[0]
    rows = C // parts
    wides = []
    for layer in range(2):
        g = (sums[layer] + products[layer]) * H
        wides.append(jnp.concatenate(
            [g[b * C : (b + 1) * C, a * C : (a + 1) * C] for a in range(3) for b in range(3)], axis=1
        ))
    for d in range(parts):
        both = [wide[d * rows : (d + 1) * rows] for wide in wides]
        grads[d] = jnp.concatenate(both, axis=0).astype(grads.dtype)


def start_kernel(ms, slopes, mine, theirs, starts):
    for i, lam in ((core(), mine), (1 - core(), theirs)):
        v = lam[...]
        for layer in (1, 0):
            v = v + slopes[layer, i] * conv(ms[layer], cols3(v))
        starts[0, i] = v


def total_kernel(parts, out):
    rows = parts.shape[1] // 2
    s = parts[0].astype(F32)
    for d in range(1, parts.shape[0]):
        s = s + parts[d].astype(F32)
    for layer in range(2):
        out[layer : layer + 1, :] = jnp.concatenate(
            [s[layer * rows + r : layer * rows + r + 1] for r in range(rows)], axis=1
        )


def call(kernel, outs, where_in, where_out, scratch, n_sems, flops, moved, grant=16 << 20):
    spaces = {"s": pltpu.SMEM, "v": pltpu.VMEM, "h": pltpu.HBM}
    specs = lambda text: [pl.BlockSpec(memory_space=spaces[k]) for k in text]
    out_specs = specs(where_out)
    return pl.pallas_call(
        kernel,
        out_shape=outs,
        in_specs=specs(where_in),
        out_specs=tuple(out_specs) if isinstance(outs, tuple) else out_specs[0],
        scratch_shapes=[pltpu.VMEM(*one) for one in scratch]
        + ([pltpu.SemaphoreType.DMA((n_sems,))] if n_sems else []),
        cost_estimate=pl.CostEstimate(flops=flops, bytes_accessed=moved, transcendentals=0),
        compiler_params=pltpu.CompilerParams(vmem_limit_bytes=grant),
    )


def shards(states, weights, guess, loss):
    sections = lax.axis_size("section")
    nb = lax.axis_size("batch")
    half = sections // 2
    chips = half // 2
    shape = jax.ShapeDtypeStruct
    image, image16 = shape((C, N), F32), shape((C, N), BF16)

    swap = [(i, i ^ 1) for i in range(sections)]
    give, keep, ms = call(
        source_kernel,
        (shape((C, 2 * N + WIDE), BF16), shape((C, 2 * N), BF16), shape((2, 3 * C, 3 * C), BF16)), "hhhh", "vvv",
        [((2, 2, C, N), BF16), ((2, C, 9 * C), BF16), ((2, C, N), F32), ((2, C, N), F32)],
        4, 6 * 10**8, 2 * 10**6, WHOLE,
    )(states, weights, guess, loss)
    got = lax.ppermute(give, "section", swap)
    pairs, odd = call(
        merge_kernel, (shape((chips, C, LEAD + N), BF16), image16), "vvv", "hv",
        [((C, LEAD + N), BF16)], 2 * chips, 10**8, 3 * 10**6,
    )(keep, got, ms)
    groups = [[x * half + 2 * y + c for y in range(chips)] for x in range(2) for c in range(2)]
    packed = lax.all_to_all(pairs, "section", 0, 0, axis_index_groups=groups, tiled=True)
    acts, slopes, base = call(
        prep_kernel, (shape((2, 2, 3 * C, N), BF16), shape((2, 2, C, N), F32), image),
        "vv", "vvv", [], 0, 10**8, 4 * 10**6,
    )(states, loss)

    last = call(upper_kernel, image16, "h", "v", [((chips, C, LEAD + N), BF16)], chips, 10**9, 2 * 10**6)(packed)
    carried = lax.ppermute(last, "section", [(i, i - half) for i in range(half, sections)])
    mine, other = call(
        lower_kernel, (image, image), "vhvv", "vv",
        [((C, N), F32), ((C, N), F32), ((chips, C, LEAD + N), BF16)], chips, 12 * 10**8, 2 * 10**6
    )(carried, packed, odd, base)
    theirs = lax.ppermute(other, "section", swap)

    sums = call(own_kernel, shape((2, 3 * C, 3 * C), F32), "vvvv", "v", [], 0, 4 * 10**8, 10**6)(ms, acts, slopes, mine)
    grads = call(
        other_kernel, shape((nb, 2 * (C // nb), 9 * C), BF16), "vvvvv", "v", [], 0, 4 * 10**8, 10**6
    )(ms, acts, slopes, theirs, sums)
    starts = call(start_kernel, shape((1, 2, C, N), F32), "vvvv", "v", [], 0, 6 * 10**8, 3 * 10**6)(
        ms, slopes, mine, theirs
    )
    grads = lax.all_to_all(grads, "batch", 0, 0, tiled=True)
    total = call(total_kernel, shape((2, 9 * C * C // nb), F32), "v", "v", [], 0, 10**6, 10**6)(grads)
    return starts, total


def solution(mesh):
    placed = (
        P("section", "batch", None, None),
        P("section", None, None),
        P("section", "batch", None, None),
        P("batch", None, None),
    )
    return jax.shard_map(
        shards,
        mesh=mesh,
        in_specs=placed,
        out_specs=(P("section", "batch", None, None), P("section", "batch")),
        check_vma=False,
    )
```

```python
import jax
import jax.numpy as jnp
from jax import lax
from jax.experimental import pallas as pl
from jax.experimental.pallas import tpu as pltpu
from jax.sharding import PartitionSpec as P


H = 0.0625
SIDE = 32
C = 64
N = SIDE * SIDE
LANES = 128
F32 = jnp.float32
BF16 = jnp.bfloat16
WIDE = 640
LEAD = 2 * N + 18 * C
WHOLE = 53 << 20


def masked(values, keep):
    return jnp.where(keep, values, jnp.zeros_like(values))


def lane(shape):
    return lax.broadcasted_iota(jnp.int32, shape, len(shape) - 1)


def cols3(v):
    v = v.astype(BF16)
    column = lane(v.shape) & (SIDE - 1)
    ahead = masked(pltpu.roll(v, N - 1, 1), column < SIDE - 1)
    behind = masked(pltpu.roll(v, 1, 1), column > 0)
    return jnp.concatenate([ahead, v, behind], axis=0)


def row_up(t):
    t = pltpu.roll(t, SIDE, 1)
    edge = t[:, :LANES]
    return jnp.concatenate([masked(edge, lane(edge.shape) >= SIDE), t[:, LANES:]], axis=1)


def row_down(t):
    t = pltpu.roll(t, N - SIDE, 1)
    edge = t[:, N - LANES :]
    return jnp.concatenate([t[:, : N - LANES], masked(edge, lane(edge.shape) < LANES - SIDE)], axis=1)


def rows3(t):
    t = t.astype(BF16)
    return jnp.concatenate([row_up(t), t, row_down(t)], axis=0)


def taps(w):
    blocks = [
        jnp.concatenate([w[:, (3 * a + b) * C : (3 * a + b + 1) * C] for a in range(3)], axis=1)
        for b in range(3)
    ]
    return jnp.concatenate(blocks, axis=0).astype(F32).T.astype(BF16)


def conv(m, x3):
    y = jnp.dot(m, x3, preferred_element_type=F32)
    low = row_down(y[:C].astype(BF16))
    high = row_up(y[2 * C :].astype(BF16))
    return y[C : 2 * C] + low.astype(F32) + high.astype(F32)


def flatten_taps(m):
    wide = [m[a * C : (a + 1) * C, : 2 * C] for a in range(3)]
    thin = [m[a * C : (a + 1) * C, 2 * C :] for a in range(3)]
    return jnp.concatenate(wide + thin, axis=1)


def pair_taps(even, odd):
    thin = [flat[:, (6 + a) * C : (7 + a) * C] for a in range(3) for flat in (even, odd)]
    return jnp.concatenate([even[:, : 6 * C], odd[:, : 6 * C]] + thin, axis=1)


def one_of_pair(pair, which):
    wide = [pair[:, (6 * which + 2 * a) * C : (6 * which + 2 * a + 2) * C] for a in range(3)]
    thin = [pair[:, (12 + 2 * a + which) * C : (13 + 2 * a + which) * C] for a in range(3)]
    return jnp.concatenate([jnp.concatenate(wide, axis=0), jnp.concatenate(thin, axis=0)], axis=1)


def core():
    return lax.rem(lax.axis_index("section"), 2)


def moves(pairs, sems, first=0):
    made = [pltpu.make_async_copy(a, b, sems.at[first + n]) for n, (a, b) in enumerate(pairs)]
    for one in made:
        one.start()
    return made


def settle(made):
    for one in made:
        one.wait()


def part_of(u, g, lc, m0, m1):
    t1 = jnp.tanh(u[1].astype(F32))
    t0 = jnp.tanh(u[0].astype(F32))
    d0 = H - H * (t0 * t0)
    t = (H - H * (t1 * t1)) * conv(m1, cols3(g))
    p = t + d0 * conv(m0, cols3(t - g + 2.0 * lc))
    return (2.0 * d0).astype(BF16), p.astype(BF16)


def source_kernel(states, weights, guess, loss, give, keep, ms, u, w, g, lc, sems):
    own = core()
    in_w, *ins = moves([(weights, w), (states, u), (guess.at[0], g), (loss, lc)], sems)
    in_w.wait()
    m1, m0 = taps(w[1]), taps(w[0])
    ms[0], ms[1] = m0, m1
    give[:, 2 * N : 2 * N + 9 * C] = flatten_taps(m0)
    give[:, 2 * N + 9 * C :] = jnp.zeros((C, WIDE - 9 * C), BF16)
    settle(ins)
    for i, out in ((1 - own, give), (own, keep)):
        out[:, :N], out[:, N : 2 * N] = part_of(u.at[:, i], g[i], lc[i], m0, m1)


def merge_kernel(keep, got, ms, out, odd, pair, sems):
    even = core() == 0
    mine, theirs = flatten_taps(ms[0]), got[:, 2 * N : 2 * N + 9 * C]
    d_even = jnp.where(even, keep[:, :N], got[:, :N])
    both = pair_taps(jnp.where(even, mine, theirs), jnp.where(even, theirs, mine))
    pair[:, :N] = d_even
    pair[:, N : 2 * N] = jnp.where(even, got[:, :N], keep[:, :N])
    pair[:, 2 * N : LEAD] = both
    chips = out.shape[0]
    sent = moves([(pair.at[:, :LEAD], out.at[k, :, :LEAD]) for k in range(chips)], sems)
    p_even = jnp.where(even, keep[:, N:], got[:, N : 2 * N])
    p_odd = jnp.where(even, got[:, N : 2 * N], keep[:, N:])
    odd[...] = p_odd
    y = conv(one_of_pair(both, 0), cols3(p_odd))
    merged = p_even.astype(F32) + p_odd.astype(F32) + d_even.astype(F32) * y
    pair[:, LEAD:] = merged.astype(BF16)
    settle(sent + moves([(pair.at[:, LEAD:], out.at[k, :, LEAD:]) for k in range(chips)], sems, chips))


def prep_kernel(states, loss, acts, slopes, base):
    base[...] = loss[core()]
    for layer in range(2):
        for i in range(2):
            t = jnp.tanh(states[layer, i].astype(F32))
            acts[layer, i] = rows3(t)
            slopes[layer, i] = H - H * (t * t)


def apply(packed, k, which, e):
    m = one_of_pair(packed[k, :, 2 * N : LEAD], which)
    return e + packed[k, :, which * N : (which + 1) * N].astype(F32) * conv(m, cols3(e))


def arrivals(source, packed, sems):
    made = [pltpu.make_async_copy(source.at[k], packed.at[k], sems.at[k]) for k in range(packed.shape[0])]
    for one in made[::-1]:
        one.start()
    return lambda k: pltpu.make_async_copy(source.at[k], packed.at[k], sems.at[k]).wait()


def upper_kernel(source, last, packed, sems):
    chips = packed.shape[0]
    arrived = arrivals(source, packed, sems)

    def step(r, e):
        k = chips - 1 - r
        arrived(k)
        x = apply(packed, k, 1, e)
        return apply(packed, k, 0, x) + packed[k, :, LEAD:].astype(F32)

    arrived(chips - 1)
    e = packed[chips - 1, :, LEAD:].astype(F32)
    last[...] = lax.fori_loop(1, chips, step, e).astype(BF16)


def lower_kernel(start, source, odd, base, mine, other, high, low, packed, sems):
    chips = packed.shape[0]
    arrived = arrivals(source, packed, sems)
    spot = lax.rem(lax.axis_index("section") // 2, chips)

    def step(r, e):
        k = chips - 1 - r
        arrived(k)
        x = apply(packed, k, 1, e)

        @pl.when(k == spot)
        def _():
            high[...] = e
            low[...] = x

        return apply(packed, k, 0, x) + packed[k, :, LEAD:].astype(F32)

    e = lax.fori_loop(0, chips - 1, step, start[...].astype(F32))
    arrived(0)
    x = apply(packed, 0, 1, e)

    @pl.when(spot == 0)
    def _():
        high[...] = e
        low[...] = x

    at_high = high[...] + base[...]
    at_low = low[...] + odd[...].astype(F32) + base[...]
    even = core() == 0
    mine[...] = jnp.where(even, at_low, at_high)
    other[...] = jnp.where(even, at_high, at_low)


def finish(i, ms, acts, slopes, v):
    x3 = cols3(v)
    first = lax.dot_general(x3, acts[1, i], (((1,), (1,)), ((), ())), preferred_element_type=F32)
    x3 = cols3(v + slopes[1, i] * conv(ms[1], x3))
    return lax.dot_general(x3, acts[0, i], (((1,), (1,)), ((), ())), preferred_element_type=F32), first


def own_kernel(ms, acts, slopes, mine, sums):
    sums[0], sums[1] = finish(core(), ms, acts, slopes, mine[...])


def other_kernel(ms, acts, slopes, other, sums, grads):
    products = finish(1 - core(), ms, acts, slopes, other[...])
    parts = grads.shape[0]
    rows = C // parts
    wides = []
    for layer in range(2):
        g = (sums[layer] + products[layer]) * H
        wides.append(jnp.concatenate(
            [g[b * C : (b + 1) * C, a * C : (a + 1) * C] for a in range(3) for b in range(3)], axis=1
        ))
    for d in range(parts):
        both = [wide[d * rows : (d + 1) * rows] for wide in wides]
        grads[d] = jnp.concatenate(both, axis=0).astype(grads.dtype)


def start_kernel(ms, slopes, mine, theirs, starts):
    for i, lam in ((core(), mine), (1 - core(), theirs)):
        v = lam[...]
        for layer in (1, 0):
            v = v + slopes[layer, i] * conv(ms[layer], cols3(v))
        starts[0, i] = v


def total_kernel(parts, out):
    rows = parts.shape[1] // 2
    s = parts[0].astype(F32)
    for d in range(1, parts.shape[0]):
        s = s + parts[d].astype(F32)
    for layer in range(2):
        out[layer : layer + 1, :] = jnp.concatenate(
            [s[layer * rows + r : layer * rows + r + 1] for r in range(rows)], axis=1
        )


def call(kernel, outs, where_in, where_out, scratch, n_sems, flops, moved, grant=16 << 20):
    spaces = {"s": pltpu.SMEM, "v": pltpu.VMEM, "h": pltpu.HBM}
    specs = lambda text: [pl.BlockSpec(memory_space=spaces[k]) for k in text]
    out_specs = specs(where_out)
    return pl.pallas_call(
        kernel,
        out_shape=outs,
        in_specs=specs(where_in),
        out_specs=tuple(out_specs) if isinstance(outs, tuple) else out_specs[0],
        scratch_shapes=[pltpu.VMEM(*one) for one in scratch]
        + ([pltpu.SemaphoreType.DMA((n_sems,))] if n_sems else []),
        cost_estimate=pl.CostEstimate(flops=flops, bytes_accessed=moved, transcendentals=0),
        compiler_params=pltpu.CompilerParams(vmem_limit_bytes=grant),
    )


def shards(states, weights, guess, loss):
    sections = lax.axis_size("section")
    nb = lax.axis_size("batch")
    half = sections // 2
    chips = half // 2
    shape = jax.ShapeDtypeStruct
    image, image16 = shape((C, N), F32), shape((C, N), BF16)

    swap = [(i, i ^ 1) for i in range(sections)]
    give, keep, ms = call(
        source_kernel,
        (shape((C, 2 * N + WIDE), BF16), shape((C, 2 * N), BF16), shape((2, 3 * C, 3 * C), BF16)), "hhhh", "vvv",
        [((2, 2, C, N), BF16), ((2, C, 9 * C), BF16), ((2, C, N), F32), ((2, C, N), F32)],
        4, 6 * 10**8, 2 * 10**6, WHOLE,
    )(states, weights, guess, loss)
    got = lax.ppermute(give, "section", swap)
    pairs, odd = call(
        merge_kernel, (shape((chips, C, LEAD + N), BF16), image16), "vvv", "hv",
        [((C, LEAD + N), BF16)], 2 * chips, 10**8, 3 * 10**6,
    )(keep, got, ms)
    groups = [[x * half + 2 * y + c for y in range(chips)] for x in range(2) for c in range(2)]
    packed = lax.all_to_all(pairs, "section", 0, 0, axis_index_groups=groups, tiled=True)
    acts, slopes, base = call(
        prep_kernel, (shape((2, 2, 3 * C, N), BF16), shape((2, 2, C, N), F32), image),
        "vv", "vvv", [], 0, 10**8, 4 * 10**6,
    )(states, loss)

    last = call(upper_kernel, image16, "h", "v", [((chips, C, LEAD + N), BF16)], chips, 10**9, 2 * 10**6)(packed)
    carried = lax.ppermute(last, "section", [(i, i - half) for i in range(half, sections)])
    mine, other = call(
        lower_kernel, (image, image), "vhvv", "vv",
        [((C, N), F32), ((C, N), F32), ((chips, C, LEAD + N), BF16)], chips, 12 * 10**8, 2 * 10**6
    )(carried, packed, odd, base)
    theirs = lax.ppermute(other, "section", swap)

    sums = call(own_kernel, shape((2, 3 * C, 3 * C), F32), "vvvv", "v", [], 0, 4 * 10**8, 10**6)(ms, acts, slopes, mine)
    grads = call(
        other_kernel, shape((nb, 2 * (C // nb), 9 * C), BF16), "vvvvv", "v", [], 0, 4 * 10**8, 10**6
    )(ms, acts, slopes, theirs, sums)
    starts = call(start_kernel, shape((1, 2, C, N), F32), "vvvv", "v", [], 0, 6 * 10**8, 3 * 10**6)(
        ms, slopes, mine, theirs
    )
    grads = lax.all_to_all(grads, "batch", 0, 0, tiled=True)
    total = call(total_kernel, shape((2, 9 * C * C // nb), F32), "v", "v", [], 0, 10**6, 10**6)(grads)
    return starts, total


def solution(mesh):
    placed = (
        P("section", "batch", None, None),
        P("section", None, None),
        P("section", "batch", None, None),
        P("batch", None, None),
    )
    return jax.shard_map(
        shards,
        mesh=mesh,
        in_specs=placed,
        out_specs=(P("section", "batch", None, None), P("section", "batch")),
        check_vma=False,
    )
```

```python
import jax
import jax.numpy as jnp
from jax import lax
from jax.experimental import pallas as pl
from jax.experimental.pallas import tpu as pltpu
from jax.sharding import PartitionSpec as P


H = 0.0625
SIDE = 32
C = 64
N = SIDE * SIDE
LANES = 128
F32 = jnp.float32
BF16 = jnp.bfloat16
WIDE = 640
LEAD = 2 * N + 18 * C
WHOLE = 53 << 20


def masked(values, keep):
    return jnp.where(keep, values, jnp.zeros_like(values))


def lane(shape):
    return lax.broadcasted_iota(jnp.int32, shape, len(shape) - 1)


def cols3(v):
    v = v.astype(BF16)
    column = lane(v.shape) & (SIDE - 1)
    ahead = masked(pltpu.roll(v, N - 1, 1), column < SIDE - 1)
    behind = masked(pltpu.roll(v, 1, 1), column > 0)
    return jnp.concatenate([ahead, v, behind], axis=0)


def row_up(t):
    t = pltpu.roll(t, SIDE, 1)
    edge = t[:, :LANES]
    return jnp.concatenate([masked(edge, lane(edge.shape) >= SIDE), t[:, LANES:]], axis=1)


def row_down(t):
    t = pltpu.roll(t, N - SIDE, 1)
    edge = t[:, N - LANES :]
    return jnp.concatenate([t[:, : N - LANES], masked(edge, lane(edge.shape) < LANES - SIDE)], axis=1)


def rows3(t):
    t = t.astype(BF16)
    return jnp.concatenate([row_up(t), t, row_down(t)], axis=0)


def taps(w):
    blocks = [
        jnp.concatenate([w[:, (3 * a + b) * C : (3 * a + b + 1) * C] for a in range(3)], axis=1)
        for b in range(3)
    ]
    return jnp.concatenate(blocks, axis=0).astype(F32).T.astype(BF16)


def conv(m, x3):
    y = jnp.dot(m, x3, preferred_element_type=F32)
    low = row_down(y[:C].astype(BF16))
    high = row_up(y[2 * C :].astype(BF16))
    return y[C : 2 * C] + low.astype(F32) + high.astype(F32)


def flatten_taps(m):
    wide = [m[a * C : (a + 1) * C, : 2 * C] for a in range(3)]
    thin = [m[a * C : (a + 1) * C, 2 * C :] for a in range(3)]
    return jnp.concatenate(wide + thin, axis=1)


def pair_taps(even, odd):
    thin = [flat[:, (6 + a) * C : (7 + a) * C] for a in range(3) for flat in (even, odd)]
    return jnp.concatenate([even[:, : 6 * C], odd[:, : 6 * C]] + thin, axis=1)


def one_of_pair(pair, which):
    wide = [pair[:, (6 * which + 2 * a) * C : (6 * which + 2 * a + 2) * C] for a in range(3)]
    thin = [pair[:, (12 + 2 * a + which) * C : (13 + 2 * a + which) * C] for a in range(3)]
    return jnp.concatenate([jnp.concatenate(wide, axis=0), jnp.concatenate(thin, axis=0)], axis=1)


def core():
    return lax.rem(lax.axis_index("section"), 2)


def moves(pairs, sems, first=0):
    made = [pltpu.make_async_copy(a, b, sems.at[first + n]) for n, (a, b) in enumerate(pairs)]
    for one in made:
        one.start()
    return made


def settle(made):
    for one in made:
        one.wait()


def part_of(u, g, lc, m0, m1):
    t1 = jnp.tanh(u[1].astype(F32))
    t0 = jnp.tanh(u[0].astype(F32))
    d0 = H - H * (t0 * t0)
    t = (H - H * (t1 * t1)) * conv(m1, cols3(g))
    p = t + d0 * conv(m0, cols3(t - g + 2.0 * lc))
    return (2.0 * d0).astype(BF16), p.astype(BF16)


def source_kernel(states, weights, guess, loss, give, keep, ms, u, w, g, lc, sems):
    own = core()
    in_w, *ins = moves([(weights, w), (states, u), (guess.at[0], g), (loss, lc)], sems)
    in_w.wait()
    m1, m0 = taps(w[1]), taps(w[0])
    ms[0], ms[1] = m0, m1
    give[:, 2 * N : 2 * N + 9 * C] = flatten_taps(m0)
    give[:, 2 * N + 9 * C :] = jnp.zeros((C, WIDE - 9 * C), BF16)
    settle(ins)
    for i, out in ((1 - own, give), (own, keep)):
        out[:, :N], out[:, N : 2 * N] = part_of(u.at[:, i], g[i], lc[i], m0, m1)


def merge_kernel(keep, got, ms, out, odd, pair, sems):
    even = core() == 0
    mine, theirs = flatten_taps(ms[0]), got[:, 2 * N : 2 * N + 9 * C]
    d_even = jnp.where(even, keep[:, :N], got[:, :N])
    both = pair_taps(jnp.where(even, mine, theirs), jnp.where(even, theirs, mine))
    pair[:, :N] = d_even
    pair[:, N : 2 * N] = jnp.where(even, got[:, :N], keep[:, :N])
    pair[:, 2 * N : LEAD] = both
    chips = out.shape[0]
    sent = moves([(pair.at[:, :LEAD], out.at[k, :, :LEAD]) for k in range(chips)], sems)
    p_even = jnp.where(even, keep[:, N:], got[:, N : 2 * N])
    p_odd = jnp.where(even, got[:, N : 2 * N], keep[:, N:])
    odd[...] = p_odd
    y = conv(one_of_pair(both, 0), cols3(p_odd))
    merged = p_even.astype(F32) + p_odd.astype(F32) + d_even.astype(F32) * y
    pair[:, LEAD:] = merged.astype(BF16)
    settle(sent + moves([(pair.at[:, LEAD:], out.at[k, :, LEAD:]) for k in range(chips)], sems, chips))


def prep_kernel(states, loss, acts, slopes, base):
    base[...] = loss[core()]
    for layer in range(2):
        for i in range(2):
            t = jnp.tanh(states[layer, i].astype(F32))
            acts[layer, i] = rows3(t)
            slopes[layer, i] = H - H * (t * t)


def apply(packed, k, which, e):
    m = one_of_pair(packed[k, :, 2 * N : LEAD], which)
    return e + packed[k, :, which * N : (which + 1) * N].astype(F32) * conv(m, cols3(e))


def arrivals(source, packed, sems):
    made = [pltpu.make_async_copy(source.at[k], packed.at[k], sems.at[k]) for k in range(packed.shape[0])]
    for one in made[::-1]:
        one.start()
    return lambda k: pltpu.make_async_copy(source.at[k], packed.at[k], sems.at[k]).wait()


def upper_kernel(source, last, packed, sems):
    chips = packed.shape[0]
    arrived = arrivals(source, packed, sems)

    def step(r, e):
        k = chips - 1 - r
        arrived(k)
        x = apply(packed, k, 1, e)
        return apply(packed, k, 0, x) + packed[k, :, LEAD:].astype(F32)

    arrived(chips - 1)
    e = packed[chips - 1, :, LEAD:].astype(F32)
    last[...] = lax.fori_loop(1, chips, step, e).astype(BF16)


def lower_kernel(start, source, odd, base, mine, other, high, low, packed, sems):
    chips = packed.shape[0]
    arrived = arrivals(source, packed, sems)
    spot = lax.rem(lax.axis_index("section") // 2, chips)

    def step(r, e):
        k = chips - 1 - r
        arrived(k)
        x = apply(packed, k, 1, e)

        @pl.when(k == spot)
        def _():
            high[...] = e
            low[...] = x

        return apply(packed, k, 0, x) + packed[k, :, LEAD:].astype(F32)

    e = lax.fori_loop(0, chips - 1, step, start[...].astype(F32))
    arrived(0)
    x = apply(packed, 0, 1, e)

    @pl.when(spot == 0)
    def _():
        high[...] = e
        low[...] = x

    at_high = high[...] + base[...]
    at_low = low[...] + odd[...].astype(F32) + base[...]
    even = core() == 0
    mine[...] = jnp.where(even, at_low, at_high)
    other[...] = jnp.where(even, at_high, at_low)


def finish(i, ms, acts, slopes, v):
    x3 = cols3(v)
    first = lax.dot_general(x3, acts[1, i], (((1,), (1,)), ((), ())), preferred_element_type=F32)
    x3 = cols3(v + slopes[1, i] * conv(ms[1], x3))
    return lax.dot_general(x3, acts[0, i], (((1,), (1,)), ((), ())), preferred_element_type=F32), first


def own_kernel(ms, acts, slopes, mine, sums):
    sums[0], sums[1] = finish(core(), ms, acts, slopes, mine[...])


def other_kernel(ms, acts, slopes, other, sums, grads):
    products = finish(1 - core(), ms, acts, slopes, other[...])
    parts = grads.shape[0]
    rows = C // parts
    wides = []
    for layer in range(2):
        g = (sums[layer] + products[layer]) * H
        wides.append(jnp.concatenate(
            [g[b * C : (b + 1) * C, a * C : (a + 1) * C] for a in range(3) for b in range(3)], axis=1
        ))
    for d in range(parts):
        both = [wide[d * rows : (d + 1) * rows] for wide in wides]
        grads[d] = jnp.concatenate(both, axis=0).astype(grads.dtype)


def start_kernel(ms, slopes, mine, theirs, starts):
    for i, lam in ((core(), mine), (1 - core(), theirs)):
        v = lam[...]
        for layer in (1, 0):
            v = v + slopes[layer, i] * conv(ms[layer], cols3(v))
        starts[0, i] = v


def total_kernel(parts, out):
    rows = parts.shape[1] // 2
    s = parts[0].astype(F32)
    for d in range(1, parts.shape[0]):
        s = s + parts[d].astype(F32)
    for layer in range(2):
        out[layer : layer + 1, :] = jnp.concatenate(
            [s[layer * rows + r : layer * rows + r + 1] for r in range(rows)], axis=1
        )


def call(kernel, outs, where_in, where_out, scratch, n_sems, flops, moved, grant=16 << 20, keep=False):
    spaces = {"s": pltpu.SMEM, "v": pltpu.VMEM, "h": pltpu.HBM}
    specs = lambda text: [pl.BlockSpec(memory_space=spaces[k]) for k in text]
    out_specs = specs(where_out)
    return pl.pallas_call(
        kernel,
        out_shape=outs,
        in_specs=specs(where_in),
        out_specs=tuple(out_specs) if isinstance(outs, tuple) else out_specs[0],
        scratch_shapes=[pltpu.VMEM(*one) for one in scratch]
        + ([pltpu.SemaphoreType.DMA((n_sems,))] if n_sems else []),
        cost_estimate=pl.CostEstimate(flops=flops, bytes_accessed=moved, transcendentals=0),
        compiler_params=pltpu.CompilerParams(vmem_limit_bytes=grant, has_side_effects=keep),
    )


def shards(states, weights, guess, loss):
    sections = lax.axis_size("section")
    nb = lax.axis_size("batch")
    half = sections // 2
    chips = half // 2
    shape = jax.ShapeDtypeStruct
    image, image16 = shape((C, N), F32), shape((C, N), BF16)

    swap = [(i, i ^ 1) for i in range(sections)]
    give, keep, ms = call(
        source_kernel,
        (shape((C, 2 * N + WIDE), BF16), shape((C, 2 * N), BF16), shape((2, 3 * C, 3 * C), BF16)), "hhhh", "vvv",
        [((2, 2, C, N), BF16), ((2, C, 9 * C), BF16), ((2, C, N), F32), ((2, C, N), F32)],
        4, 6 * 10**8, 2 * 10**6, WHOLE,
    )(states, weights, guess, loss)
    got = lax.ppermute(give, "section", swap)
    pairs, odd = call(
        merge_kernel, (shape((chips, C, LEAD + N), BF16), image16), "vvv", "hv",
        [((C, LEAD + N), BF16)], 2 * chips, 10**8, 3 * 10**6,
    )(keep, got, ms)
    groups = [[x * half + 2 * y + c for y in range(chips)] for x in range(2) for c in range(2)]
    packed = lax.all_to_all(pairs, "section", 0, 0, axis_index_groups=groups, tiled=True)
    acts, slopes, base = call(
        prep_kernel, (shape((2, 2, 3 * C, N), BF16), shape((2, 2, C, N), F32), image),
        "vv", "vvv", [], 0, 10**8, 4 * 10**6,
    )(states, loss)

    upper = call(upper_kernel, image16, "h", "v", [((chips, C, LEAD + N), BF16)], chips, 10**9, 2 * 10**6, keep=True)
    lower = call(
        lower_kernel, (image, image), "vhvv", "vv",
        [((C, N), F32), ((C, N), F32), ((chips, C, LEAD + N), BF16)], chips, 12 * 10**8, 2 * 10**6, keep=True,
    )
    own = call(own_kernel, shape((2, 3 * C, 3 * C), F32), "vvvv", "v", [], 0, 4 * 10**8, 10**6, keep=True)
    rest = call(other_kernel, shape((nb, 2 * (C // nb), 9 * C), BF16), "vvvvv", "v", [], 0, 4 * 10**8, 10**6, keep=True)
    total = call(total_kernel, shape((2, 9 * C * C // nb), F32), "v", "v", [], 0, 10**6, 10**6)

    near, far = lower(upper(pairs), pairs, odd, base)
    rest(ms, acts, slopes, far, own(ms, acts, slopes, near))

    last = upper(packed)
    carried = lax.ppermute(last, "section", [(i, i - half) for i in range(half, sections)])
    mine, other = lower(carried, packed, odd, base)
    theirs = lax.ppermute(other, "section", swap)
    sums = own(ms, acts, slopes, mine)
    grads = rest(ms, acts, slopes, theirs, sums)
    starts = call(start_kernel, shape((1, 2, C, N), F32), "vvvv", "v", [], 0, 6 * 10**8, 3 * 10**6)(
        ms, slopes, mine, theirs
    )
    grads = lax.all_to_all(grads, "batch", 0, 0, tiled=True)
    return starts, total(grads)


def solution(mesh):
    placed = (
        P("section", "batch", None, None),
        P("section", None, None),
        P("section", "batch", None, None),
        P("batch", None, None),
    )
    return jax.shard_map(
        shards,
        mesh=mesh,
        in_specs=placed,
        out_specs=(P("section", "batch", None, None), P("section", "batch")),
        check_vma=False,
    )
```

```python
import jax
import jax.numpy as jnp
from jax import lax
from jax.experimental import pallas as pl
from jax.experimental.pallas import tpu as pltpu
from jax.sharding import PartitionSpec as P


H = 0.0625
SIDE = 32
C = 64
N = SIDE * SIDE
LANES = 128
F32 = jnp.float32
BF16 = jnp.bfloat16
WIDE = 640
LEAD = 2 * N + 18 * C


def masked(values, keep):
    return jnp.where(keep, values, jnp.zeros_like(values))


def lane(shape):
    return lax.broadcasted_iota(jnp.int32, shape, len(shape) - 1)


def cols3(v):
    v = v.astype(BF16)
    column = lane(v.shape) & (SIDE - 1)
    ahead = masked(pltpu.roll(v, N - 1, 1), column < SIDE - 1)
    behind = masked(pltpu.roll(v, 1, 1), column > 0)
    return jnp.concatenate([ahead, v, behind], axis=0)


def row_up(t):
    t = pltpu.roll(t, SIDE, 1)
    edge = t[:, :LANES]
    return jnp.concatenate([masked(edge, lane(edge.shape) >= SIDE), t[:, LANES:]], axis=1)


def row_down(t):
    t = pltpu.roll(t, N - SIDE, 1)
    edge = t[:, N - LANES :]
    return jnp.concatenate([t[:, : N - LANES], masked(edge, lane(edge.shape) < LANES - SIDE)], axis=1)


def rows3(t):
    t = t.astype(BF16)
    return jnp.concatenate([row_up(t), t, row_down(t)], axis=0)


def taps(w):
    blocks = [
        jnp.concatenate([w[:, (3 * a + b) * C : (3 * a + b + 1) * C] for a in range(3)], axis=1)
        for b in range(3)
    ]
    return jnp.concatenate(blocks, axis=0).astype(F32).T.astype(BF16)


def conv(m, x3):
    y = jnp.dot(m, x3, preferred_element_type=F32)
    low = row_down(y[:C].astype(BF16))
    high = row_up(y[2 * C :].astype(BF16))
    return y[C : 2 * C] + low.astype(F32) + high.astype(F32)


def flatten_taps(m):
    wide = [m[a * C : (a + 1) * C, : 2 * C] for a in range(3)]
    thin = [m[a * C : (a + 1) * C, 2 * C :] for a in range(3)]
    return jnp.concatenate(wide + thin, axis=1)


def pair_taps(even, odd):
    thin = [flat[:, (6 + a) * C : (7 + a) * C] for a in range(3) for flat in (even, odd)]
    return jnp.concatenate([even[:, : 6 * C], odd[:, : 6 * C]] + thin, axis=1)


def one_of_pair(pair, which):
    wide = [pair[:, (6 * which + 2 * a) * C : (6 * which + 2 * a + 2) * C] for a in range(3)]
    thin = [pair[:, (12 + 2 * a + which) * C : (13 + 2 * a + which) * C] for a in range(3)]
    return jnp.concatenate([jnp.concatenate(wide, axis=0), jnp.concatenate(thin, axis=0)], axis=1)


def core():
    return lax.rem(lax.axis_index("section"), 2)


def moves(pairs, sems, first=0):
    made = [pltpu.make_async_copy(a, b, sems.at[first + n]) for n, (a, b) in enumerate(pairs)]
    for one in made:
        one.start()
    return made


def settle(made):
    for one in made:
        one.wait()


def part_of(u, g, lc, m0, m1):
    t1 = jnp.tanh(u[1].astype(F32))
    t0 = jnp.tanh(u[0].astype(F32))
    d0 = H - H * (t0 * t0)
    t = (H - H * (t1 * t1)) * conv(m1, cols3(g))
    p = t + d0 * conv(m0, cols3(t - g + 2.0 * lc))
    return (2.0 * d0).astype(BF16), p.astype(BF16)


def source_kernel(states, weights, guess, loss, give, keep, ms, u, w, g, lc, sems):
    own = core()
    in_w, *ins = moves([(weights, w), (states, u), (guess.at[0], g), (loss, lc)], sems)
    in_w.wait()
    m1, m0 = taps(w[1]), taps(w[0])
    ms[0], ms[1] = m0, m1
    give[:, 2 * N : 2 * N + 9 * C] = flatten_taps(m0)
    give[:, 2 * N + 9 * C :] = jnp.zeros((C, WIDE - 9 * C), BF16)
    settle(ins)
    for i, out in ((1 - own, give), (own, keep)):
        out[:, :N], out[:, N : 2 * N] = part_of(u.at[:, i], g[i], lc[i], m0, m1)


def merge_kernel(keep, got, ms, out, odd):
    even = core() == 0
    mine, theirs = flatten_taps(ms[0]), got[:, 2 * N : 2 * N + 9 * C]
    both = pair_taps(jnp.where(even, mine, theirs), jnp.where(even, theirs, mine))
    d_even = jnp.where(even, keep[:, :N], got[:, :N])
    d_odd = jnp.where(even, got[:, :N], keep[:, :N])
    p_even = jnp.where(even, keep[:, N:], got[:, N : 2 * N])
    p_odd = jnp.where(even, got[:, N : 2 * N], keep[:, N:])
    odd[...] = p_odd
    y = conv(one_of_pair(both, 0), cols3(p_odd))
    merged = (p_even.astype(F32) + p_odd.astype(F32) + d_even.astype(F32) * y).astype(BF16)
    for k in range(out.shape[0]):
        out[k, :, :N] = d_even
        out[k, :, N : 2 * N] = d_odd
        out[k, :, 2 * N : LEAD] = both
        out[k, :, LEAD:] = merged


def prep_kernel(states, loss, acts, slopes, base):
    base[...] = loss[core()]
    for layer in range(2):
        for i in range(2):
            t = jnp.tanh(states[layer, i].astype(F32))
            acts[layer, i] = rows3(t)
            slopes[layer, i] = H - H * (t * t)


def apply(packed, k, which, e):
    m = one_of_pair(packed[k, :, 2 * N : LEAD], which)
    return e + packed[k, :, which * N : (which + 1) * N].astype(F32) * conv(m, cols3(e))


def upper_kernel(packed, last):
    chips = packed.shape[0]

    def step(r, e):
        k = chips - 1 - r
        x = apply(packed, k, 1, e)
        return apply(packed, k, 0, x) + packed[k, :, LEAD:].astype(F32)

    e = packed[chips - 1, :, LEAD:].astype(F32)
    last[...] = lax.fori_loop(1, chips, step, e).astype(BF16)


def lower_kernel(start, packed, odd, base, mine, other, high, low):
    chips = packed.shape[0]
    spot = lax.rem(lax.axis_index("section") // 2, chips)

    def step(r, e):
        k = chips - 1 - r
        x = apply(packed, k, 1, e)

        @pl.when(k == spot)
        def _():
            high[...] = e
            low[...] = x

        return apply(packed, k, 0, x) + packed[k, :, LEAD:].astype(F32)

    e = lax.fori_loop(0, chips - 1, step, start[...].astype(F32))
    x = apply(packed, 0, 1, e)

    @pl.when(spot == 0)
    def _():
        high[...] = e
        low[...] = x

    at_high = high[...] + base[...]
    at_low = low[...] + odd[...].astype(F32) + base[...]
    even = core() == 0
    mine[...] = jnp.where(even, at_low, at_high)
    other[...] = jnp.where(even, at_high, at_low)


def finish(i, ms, acts, slopes, v):
    x3 = cols3(v)
    first = lax.dot_general(x3, acts[1, i], (((1,), (1,)), ((), ())), preferred_element_type=F32)
    x3 = cols3(v + slopes[1, i] * conv(ms[1], x3))
    return lax.dot_general(x3, acts[0, i], (((1,), (1,)), ((), ())), preferred_element_type=F32), first


def own_kernel(ms, acts, slopes, mine, sums):
    sums[0], sums[1] = finish(core(), ms, acts, slopes, mine[...])


def other_kernel(ms, acts, slopes, other, sums, grads):
    products = finish(1 - core(), ms, acts, slopes, other[...])
    parts = grads.shape[0]
    rows = C // parts
    wides = []
    for layer in range(2):
        g = (sums[layer] + products[layer]) * H
        wides.append(jnp.concatenate(
            [g[b * C : (b + 1) * C, a * C : (a + 1) * C] for a in range(3) for b in range(3)], axis=1
        ))
    for d in range(parts):
        both = [wide[d * rows : (d + 1) * rows] for wide in wides]
        grads[d] = jnp.concatenate(both, axis=0).astype(grads.dtype)


def start_kernel(ms, slopes, mine, theirs, starts):
    for i, lam in ((core(), mine), (1 - core(), theirs)):
        v = lam[...]
        for layer in (1, 0):
            v = v + slopes[layer, i] * conv(ms[layer], cols3(v))
        starts[0, i] = v


def total_kernel(parts, out):
    rows = parts.shape[1] // 2
    s = parts[0].astype(F32)
    for d in range(1, parts.shape[0]):
        s = s + parts[d].astype(F32)
    for layer in range(2):
        out[layer : layer + 1, :] = jnp.concatenate(
            [s[layer * rows + r : layer * rows + r + 1] for r in range(rows)], axis=1
        )


def call(kernel, outs, where_in, where_out, scratch, n_sems, flops, moved, grant=16 << 20):
    spaces = {"s": pltpu.SMEM, "v": pltpu.VMEM, "h": pltpu.HBM}
    specs = lambda text: [pl.BlockSpec(memory_space=spaces[k]) for k in text]
    out_specs = specs(where_out)
    return pl.pallas_call(
        kernel,
        out_shape=outs,
        in_specs=specs(where_in),
        out_specs=tuple(out_specs) if isinstance(outs, tuple) else out_specs[0],
        scratch_shapes=[pltpu.VMEM(*one) for one in scratch]
        + ([pltpu.SemaphoreType.DMA((n_sems,))] if n_sems else []),
        cost_estimate=pl.CostEstimate(flops=flops, bytes_accessed=moved, transcendentals=0),
        compiler_params=pltpu.CompilerParams(vmem_limit_bytes=grant),
    )


def shards(states, weights, guess, loss):
    sections = lax.axis_size("section")
    nb = lax.axis_size("batch")
    half = sections // 2
    chips = half // 2
    shape = jax.ShapeDtypeStruct
    image, image16 = shape((C, N), F32), shape((C, N), BF16)

    swap = [(i, i ^ 1) for i in range(sections)]
    give, keep, ms = call(
        source_kernel,
        (shape((C, 2 * N + WIDE), BF16), shape((C, 2 * N), BF16), shape((2, 3 * C, 3 * C), BF16)), "hhhh", "vvv",
        [((2, 2, C, N), BF16), ((2, C, 9 * C), BF16), ((2, C, N), F32), ((2, C, N), F32)],
        4, 6 * 10**8, 2 * 10**6,
    )(*[pltpu.with_memory_space_constraint(x, pltpu.HBM) for x in (states, weights, guess, loss)])
    got = lax.ppermute(give, "section", swap)
    pairs, odd = call(
        merge_kernel, (shape((chips, C, LEAD + N), BF16), image16), "vvv", "vv", [], 0, 10**8, 3 * 10**6,
    )(keep, got, ms)
    groups = [[x * half + 2 * y + c for y in range(chips)] for x in range(2) for c in range(2)]
    packed = lax.all_to_all(pairs, "section", 0, 0, axis_index_groups=groups, tiled=True)
    acts, slopes, base = call(
        prep_kernel, (shape((2, 2, 3 * C, N), BF16), shape((2, 2, C, N), F32), image),
        "vv", "vvv", [], 0, 10**8, 4 * 10**6,
    )(states, loss)

    last = call(upper_kernel, image16, "v", "v", [], 0, 10**9, 2 * 10**6)(packed)
    carried = lax.ppermute(last, "section", [(i, i - half) for i in range(half, sections)])
    mine, other = call(
        lower_kernel, (image, image), "vvvv", "vv",
        [((C, N), F32), ((C, N), F32)], 0, 12 * 10**8, 2 * 10**6
    )(carried, packed, odd, base)
    theirs = lax.ppermute(other, "section", swap)

    sums = call(own_kernel, shape((2, 3 * C, 3 * C), F32), "vvvv", "v", [], 0, 4 * 10**8, 10**6)(ms, acts, slopes, mine)
    grads = call(
        other_kernel, shape((nb, 2 * (C // nb), 9 * C), BF16), "vvvvv", "v", [], 0, 4 * 10**8, 10**6
    )(ms, acts, slopes, theirs, sums)
    starts = call(start_kernel, shape((1, 2, C, N), F32), "vvvv", "v", [], 0, 6 * 10**8, 3 * 10**6)(
        ms, slopes, mine, theirs
    )
    grads = lax.all_to_all(grads, "batch", 0, 0, tiled=True)
    total = call(total_kernel, shape((2, 9 * C * C // nb), F32), "v", "v", [], 0, 10**6, 10**6)(grads)
    return starts, total


def solution(mesh):
    placed = (
        P("section", "batch", None, None),
        P("section", None, None),
        P("section", "batch", None, None),
        P("batch", None, None),
    )
    return jax.shard_map(
        shards,
        mesh=mesh,
        in_specs=placed,
        out_specs=(P("section", "batch", None, None), P("section", "batch")),
        check_vma=False,
    )
```

```python
import jax
import jax.numpy as jnp
from jax import lax
from jax.experimental import pallas as pl
from jax.experimental.pallas import tpu as pltpu
from jax.sharding import PartitionSpec as P


H = 0.0625
SIDE = 32
C = 64
N = SIDE * SIDE
LANES = 128
F32 = jnp.float32
BF16 = jnp.bfloat16
WIDE = 640
LEAD = 2 * N + 18 * C


def masked(values, keep):
    return jnp.where(keep, values, jnp.zeros_like(values))


def lane(shape):
    return lax.broadcasted_iota(jnp.int32, shape, len(shape) - 1)


def cols3(v):
    v = v.astype(BF16)
    column = lane(v.shape) & (SIDE - 1)
    ahead = masked(pltpu.roll(v, N - 1, 1), column < SIDE - 1)
    behind = masked(pltpu.roll(v, 1, 1), column > 0)
    return jnp.concatenate([ahead, v, behind], axis=0)


def row_up(t):
    t = pltpu.roll(t, SIDE, 1)
    edge = t[:, :LANES]
    return jnp.concatenate([masked(edge, lane(edge.shape) >= SIDE), t[:, LANES:]], axis=1)


def row_down(t):
    t = pltpu.roll(t, N - SIDE, 1)
    edge = t[:, N - LANES :]
    return jnp.concatenate([t[:, : N - LANES], masked(edge, lane(edge.shape) < LANES - SIDE)], axis=1)


def rows3(t):
    t = t.astype(BF16)
    return jnp.concatenate([row_up(t), t, row_down(t)], axis=0)


def taps(w):
    blocks = [
        jnp.concatenate([w[:, (3 * a + b) * C : (3 * a + b + 1) * C] for a in range(3)], axis=1)
        for b in range(3)
    ]
    return jnp.concatenate(blocks, axis=0).astype(F32).T.astype(BF16)


def conv(m, x3):
    y = jnp.dot(m, x3, preferred_element_type=F32)
    low = row_down(y[:C].astype(BF16))
    high = row_up(y[2 * C :].astype(BF16))
    return y[C : 2 * C] + low.astype(F32) + high.astype(F32)


def flatten_taps(m):
    wide = [m[a * C : (a + 1) * C, : 2 * C] for a in range(3)]
    thin = [m[a * C : (a + 1) * C, 2 * C :] for a in range(3)]
    return jnp.concatenate(wide + thin, axis=1)


def pair_taps(even, odd):
    thin = [flat[:, (6 + a) * C : (7 + a) * C] for a in range(3) for flat in (even, odd)]
    return jnp.concatenate([even[:, : 6 * C], odd[:, : 6 * C]] + thin, axis=1)


def one_of_pair(pair, which):
    wide = [pair[:, (6 * which + 2 * a) * C : (6 * which + 2 * a + 2) * C] for a in range(3)]
    thin = [pair[:, (12 + 2 * a + which) * C : (13 + 2 * a + which) * C] for a in range(3)]
    return jnp.concatenate([jnp.concatenate(wide, axis=0), jnp.concatenate(thin, axis=0)], axis=1)


def core():
    return lax.rem(lax.axis_index("section"), 2)


def moves(pairs, sems, first=0):
    made = [pltpu.make_async_copy(a, b, sems.at[first + n]) for n, (a, b) in enumerate(pairs)]
    for one in made:
        one.start()
    return made


def settle(made):
    for one in made:
        one.wait()


def part_of(u, g, lc, m0, m1):
    t1 = jnp.tanh(u[1].astype(F32))
    t0 = jnp.tanh(u[0].astype(F32))
    d0 = H - H * (t0 * t0)
    t = (H - H * (t1 * t1)) * conv(m1, cols3(g))
    p = t + d0 * conv(m0, cols3(t - g + 2.0 * lc))
    return (2.0 * d0).astype(BF16), p.astype(BF16)


def give_kernel(states, weights, guess, loss, give, ms, u, g, lc, w, u_give, g_give, lc_give, sems):
    own = core()
    other = 1 - own
    in_w, *first = moves(
        [(weights, w), (states.at[0, other], u_give.at[0]), (states.at[1, other], u_give.at[1]),
         (guess.at[0, other], g_give), (loss.at[other], lc_give)],
        sems,
    )
    second = moves(
        [(states.at[0, own], u.at[0]), (states.at[1, own], u.at[1]), (guess.at[0, own], g), (loss.at[own], lc)],
        sems, 5,
    )
    in_w.wait()
    m1, m0 = taps(w[1]), taps(w[0])
    ms[0], ms[1] = m0, m1
    give[:, 2 * N : 2 * N + 9 * C] = flatten_taps(m0)
    give[:, 2 * N + 9 * C :] = jnp.zeros((C, WIDE - 9 * C), BF16)
    settle(first)
    give[:, :N], give[:, N : 2 * N] = part_of(u_give, g_give[...], lc_give[...], m0, m1)
    settle(second)


def keep_kernel(ms, u, g, lc, keep):
    keep[:, :N], keep[:, N:] = part_of(u, g[...], lc[...], ms[0], ms[1])


def merge_kernel(keep, got, ms, out, odd):
    even = core() == 0
    mine, theirs = flatten_taps(ms[0]), got[:, 2 * N : 2 * N + 9 * C]
    both = pair_taps(jnp.where(even, mine, theirs), jnp.where(even, theirs, mine))
    d_even = jnp.where(even, keep[:, :N], got[:, :N])
    d_odd = jnp.where(even, got[:, :N], keep[:, :N])
    p_even = jnp.where(even, keep[:, N:], got[:, N : 2 * N])
    p_odd = jnp.where(even, got[:, N : 2 * N], keep[:, N:])
    odd[...] = p_odd
    y = conv(one_of_pair(both, 0), cols3(p_odd))
    merged = (p_even.astype(F32) + p_odd.astype(F32) + d_even.astype(F32) * y).astype(BF16)
    for k in range(out.shape[0]):
        out[k, :, :N] = d_even
        out[k, :, N : 2 * N] = d_odd
        out[k, :, 2 * N : LEAD] = both
        out[k, :, LEAD:] = merged


def prep_kernel(states, loss, acts, slopes, base):
    base[...] = loss[core()]
    for layer in range(2):
        for i in range(2):
            t = jnp.tanh(states[layer, i].astype(F32))
            acts[layer, i] = rows3(t)
            slopes[layer, i] = H - H * (t * t)


def apply(packed, k, which, e):
    m = one_of_pair(packed[k, :, 2 * N : LEAD], which)
    return e + packed[k, :, which * N : (which + 1) * N].astype(F32) * conv(m, cols3(e))


def upper_kernel(packed, last):
    chips = packed.shape[0]

    def step(r, e):
        k = chips - 1 - r
        x = apply(packed, k, 1, e)
        return apply(packed, k, 0, x) + packed[k, :, LEAD:].astype(F32)

    e = packed[chips - 1, :, LEAD:].astype(F32)
    last[...] = lax.fori_loop(1, chips, step, e).astype(BF16)


def lower_kernel(start, packed, odd, base, mine, other, high, low):
    chips = packed.shape[0]
    spot = lax.rem(lax.axis_index("section") // 2, chips)

    def step(r, e):
        k = chips - 1 - r
        x = apply(packed, k, 1, e)

        @pl.when(k == spot)
        def _():
            high[...] = e
            low[...] = x

        return apply(packed, k, 0, x) + packed[k, :, LEAD:].astype(F32)

    e = lax.fori_loop(0, chips - 1, step, start[...].astype(F32))
    x = apply(packed, 0, 1, e)

    @pl.when(spot == 0)
    def _():
        high[...] = e
        low[...] = x

    at_high = high[...] + base[...]
    at_low = low[...] + odd[...].astype(F32) + base[...]
    even = core() == 0
    mine[...] = jnp.where(even, at_low, at_high)
    other[...] = jnp.where(even, at_high, at_low)


def finish(i, ms, acts, slopes, v):
    x3 = cols3(v)
    first = lax.dot_general(x3, acts[1, i], (((1,), (1,)), ((), ())), preferred_element_type=F32)
    x3 = cols3(v + slopes[1, i] * conv(ms[1], x3))
    return lax.dot_general(x3, acts[0, i], (((1,), (1,)), ((), ())), preferred_element_type=F32), first


def own_kernel(ms, acts, slopes, mine, sums):
    sums[0], sums[1] = finish(core(), ms, acts, slopes, mine[...])


def other_kernel(ms, acts, slopes, other, sums, grads):
    products = finish(1 - core(), ms, acts, slopes, other[...])
    parts = grads.shape[0]
    rows = C // parts
    g = [(sums[layer] + products[layer]) * H for layer in range(2)]
    cut = 2 * C
    rest = jnp.concatenate([g[0][:, cut:], g[1][:, cut:]], axis=1)
    for d in range(parts):
        pieces = [
            piece[b * C + d * rows : b * C + (d + 1) * rows]
            for piece in (g[0][:, :cut], g[1][:, :cut], rest) for b in range(3)
        ]
        grads[d] = jnp.concatenate(pieces, axis=0).astype(grads.dtype)


def start_kernel(ms, slopes, mine, theirs, starts):
    for i, lam in ((core(), mine), (1 - core(), theirs)):
        v = lam[...]
        for layer in (1, 0):
            v = v + slopes[layer, i] * conv(ms[layer], cols3(v))
        starts[0, i] = v


def total_kernel(parts, out):
    rows = parts.shape[1] // 9
    s = parts[0].astype(F32)
    for d in range(1, parts.shape[0]):
        s = s + parts[d].astype(F32)

    def tap(layer, a, b):
        block, start = (2, layer * C) if a == 2 else (layer, a * C)
        return s[(3 * block + b) * rows : (3 * block + b + 1) * rows, start : start + C]

    for layer in range(2):
        wide = jnp.concatenate([tap(layer, a, b) for a in range(3) for b in range(3)], axis=1)
        out[layer : layer + 1, :] = jnp.concatenate([wide[r : r + 1] for r in range(rows)], axis=1)


def call(kernel, outs, where_in, where_out, scratch, n_sems, flops, moved, grant=16 << 20):
    spaces = {"s": pltpu.SMEM, "v": pltpu.VMEM, "h": pltpu.HBM}
    specs = lambda text: [pl.BlockSpec(memory_space=spaces[k]) for k in text]
    out_specs = specs(where_out)
    return pl.pallas_call(
        kernel,
        out_shape=outs,
        in_specs=specs(where_in),
        out_specs=tuple(out_specs) if isinstance(outs, tuple) else out_specs[0],
        scratch_shapes=[pltpu.VMEM(*one) for one in scratch]
        + ([pltpu.SemaphoreType.DMA((n_sems,))] if n_sems else []),
        cost_estimate=pl.CostEstimate(flops=flops, bytes_accessed=moved, transcendentals=0),
        compiler_params=pltpu.CompilerParams(vmem_limit_bytes=grant),
    )


def shards(states, weights, guess, loss):
    sections = lax.axis_size("section")
    nb = lax.axis_size("batch")
    half = sections // 2
    chips = half // 2
    shape = jax.ShapeDtypeStruct
    image, image16 = shape((C, N), F32), shape((C, N), BF16)

    swap = [(i, i ^ 1) for i in range(sections)]
    give, ms, u, g, lc = call(
        give_kernel,
        (shape((C, 2 * N + WIDE), BF16), shape((2, 3 * C, 3 * C), BF16), shape((2, C, N), BF16), image, image),
        "hhhh", "vvvvv", [((2, C, 9 * C), BF16), ((2, C, N), BF16), ((C, N), F32), ((C, N), F32)],
        9, 3 * 10**8, 2 * 10**6,
    )(*[pltpu.with_memory_space_constraint(x, pltpu.HBM) for x in (states, weights, guess, loss)])
    got = lax.ppermute(give, "section", swap)
    keep = call(keep_kernel, shape((C, 2 * N), BF16), "vvvv", "v", [], 0, 3 * 10**8, 10**6)(ms, u, g, lc)
    pairs, odd = call(
        merge_kernel, (shape((chips, C, LEAD + N), BF16), image16), "vvv", "vv", [], 0, 10**8, 3 * 10**6,
    )(keep, got, ms)
    groups = [[x * half + 2 * y + c for y in range(chips)] for x in range(2) for c in range(2)]
    packed = lax.all_to_all(pairs, "section", 0, 0, axis_index_groups=groups, tiled=True)
    acts, slopes, base = call(
        prep_kernel, (shape((2, 2, 3 * C, N), BF16), shape((2, 2, C, N), F32), image),
        "vv", "vvv", [], 0, 10**8, 4 * 10**6,
    )(states, loss)

    last = call(upper_kernel, image16, "v", "v", [], 0, 10**9, 2 * 10**6)(packed)
    carried = lax.ppermute(last, "section", [(i, i - half) for i in range(half, sections)])
    mine, other = call(
        lower_kernel, (image, image), "vvvv", "vv",
        [((C, N), F32), ((C, N), F32)], 0, 12 * 10**8, 2 * 10**6
    )(carried, packed, odd, base)
    theirs = lax.ppermute(other, "section", swap)

    sums = call(own_kernel, shape((2, 3 * C, 3 * C), F32), "vvvv", "v", [], 0, 4 * 10**8, 10**6)(ms, acts, slopes, mine)
    grads = call(
        other_kernel, shape((nb, 9 * (C // nb), 2 * C), BF16), "vvvvv", "v", [], 0, 4 * 10**8, 10**6
    )(ms, acts, slopes, theirs, sums)
    starts = call(start_kernel, shape((1, 2, C, N), F32), "vvvv", "v", [], 0, 6 * 10**8, 3 * 10**6)(
        ms, slopes, mine, theirs
    )
    grads = lax.all_to_all(grads, "batch", 0, 0, tiled=True)
    total = call(total_kernel, shape((2, 9 * C * C // nb), F32), "v", "v", [], 0, 10**6, 10**6)(grads)
    return starts, total


def solution(mesh):
    placed = (
        P("section", "batch", None, None),
        P("section", None, None),
        P("section", "batch", None, None),
        P("batch", None, None),
    )
    return jax.shard_map(
        shards,
        mesh=mesh,
        in_specs=placed,
        out_specs=(P("section", "batch", None, None), P("section", "batch")),
        check_vma=False,
    )
```

```python
import jax
import jax.numpy as jnp
from jax import lax
from jax.experimental import pallas as pl
from jax.experimental.pallas import tpu as pltpu
from jax.sharding import PartitionSpec as P


H = 0.0625
SIDE = 32
C = 64
N = SIDE * SIDE
LANES = 128
F32 = jnp.float32
BF16 = jnp.bfloat16
WIDE = 640
LEAD = 2 * N + 18 * C


def masked(values, keep):
    return jnp.where(keep, values, jnp.zeros_like(values))


def lane(shape):
    return lax.broadcasted_iota(jnp.int32, shape, len(shape) - 1)


def cols3(v):
    v = v.astype(BF16)
    column = lane(v.shape) & (SIDE - 1)
    ahead = masked(pltpu.roll(v, N - 1, 1), column < SIDE - 1)
    behind = masked(pltpu.roll(v, 1, 1), column > 0)
    return jnp.concatenate([ahead, v, behind], axis=0)


def row_up(t):
    t = pltpu.roll(t, SIDE, 1)
    edge = t[:, :LANES]
    return jnp.concatenate([masked(edge, lane(edge.shape) >= SIDE), t[:, LANES:]], axis=1)


def row_down(t):
    t = pltpu.roll(t, N - SIDE, 1)
    edge = t[:, N - LANES :]
    return jnp.concatenate([t[:, : N - LANES], masked(edge, lane(edge.shape) < LANES - SIDE)], axis=1)


def rows3(t):
    t = t.astype(BF16)
    return jnp.concatenate([row_up(t), t, row_down(t)], axis=0)


def taps(w):
    blocks = [
        jnp.concatenate([w[:, (3 * a + b) * C : (3 * a + b + 1) * C] for a in range(3)], axis=1)
        for b in range(3)
    ]
    return jnp.concatenate(blocks, axis=0).astype(F32).T.astype(BF16)


def conv(m, x3):
    y = jnp.dot(m, x3, preferred_element_type=F32)
    low = row_down(y[:C].astype(BF16))
    high = row_up(y[2 * C :].astype(BF16))
    return y[C : 2 * C] + low.astype(F32) + high.astype(F32)


def flatten_taps(m):
    wide = [m[a * C : (a + 1) * C, : 2 * C] for a in range(3)]
    thin = [m[a * C : (a + 1) * C, 2 * C :] for a in range(3)]
    return jnp.concatenate(wide + thin, axis=1)


def pair_taps(even, odd):
    thin = [flat[:, (6 + a) * C : (7 + a) * C] for a in range(3) for flat in (even, odd)]
    return jnp.concatenate([even[:, : 6 * C], odd[:, : 6 * C]] + thin, axis=1)


def one_of_pair(pair, which):
    wide = [pair[:, (6 * which + 2 * a) * C : (6 * which + 2 * a + 2) * C] for a in range(3)]
    thin = [pair[:, (12 + 2 * a + which) * C : (13 + 2 * a + which) * C] for a in range(3)]
    return jnp.concatenate([jnp.concatenate(wide, axis=0), jnp.concatenate(thin, axis=0)], axis=1)


def core():
    return lax.rem(lax.axis_index("section"), 2)


def moves(pairs, sems, first=0):
    made = [pltpu.make_async_copy(a, b, sems.at[first + n]) for n, (a, b) in enumerate(pairs)]
    for one in made:
        one.start()
    return made


def settle(made):
    for one in made:
        one.wait()


def part_of(u, g, lc, m0, m1):
    t1 = jnp.tanh(u[1].astype(F32))
    t0 = jnp.tanh(u[0].astype(F32))
    d0 = H - H * (t0 * t0)
    t = (H - H * (t1 * t1)) * conv(m1, cols3(g))
    p = t + d0 * conv(m0, cols3(t - g + 2.0 * lc))
    return (2.0 * d0).astype(BF16), p.astype(BF16)


def give_kernel(states, weights, guess, loss, give, ms, u, g, lc, w, u_give, g_give, lc_give, sems):
    own = core()
    other = 1 - own
    in_w, *first = moves(
        [(weights, w), (states.at[0, other], u_give.at[0]), (states.at[1, other], u_give.at[1]),
         (guess.at[0, other], g_give), (loss.at[other], lc_give)],
        sems,
    )
    second = moves(
        [(states.at[0, own], u.at[0]), (states.at[1, own], u.at[1]), (guess.at[0, own], g), (loss.at[own], lc)],
        sems, 5,
    )
    in_w.wait()
    m1, m0 = taps(w[1]), taps(w[0])
    ms[0], ms[1] = m0, m1
    give[:, 2 * N : 2 * N + 9 * C] = flatten_taps(m0)
    give[:, 2 * N + 9 * C :] = jnp.zeros((C, WIDE - 9 * C), BF16)
    settle(first)
    give[:, :N], give[:, N : 2 * N] = part_of(u_give, g_give[...], lc_give[...], m0, m1)
    settle(second)


def keep_kernel(ms, u, g, lc, keep):
    keep[:, :N], keep[:, N:] = part_of(u, g[...], lc[...], ms[0], ms[1])


def merge_kernel(keep, got, ms, out, odd):
    even = core() == 0
    mine, theirs = flatten_taps(ms[0]), got[:, 2 * N : 2 * N + 9 * C]
    both = pair_taps(jnp.where(even, mine, theirs), jnp.where(even, theirs, mine))
    d_even = jnp.where(even, keep[:, :N], got[:, :N])
    d_odd = jnp.where(even, got[:, :N], keep[:, :N])
    p_even = jnp.where(even, keep[:, N:], got[:, N : 2 * N])
    p_odd = jnp.where(even, got[:, N : 2 * N], keep[:, N:])
    odd[...] = p_odd
    y = conv(one_of_pair(both, 0), cols3(p_odd))
    merged = (p_even.astype(F32) + p_odd.astype(F32) + d_even.astype(F32) * y).astype(BF16)
    for k in range(out.shape[0]):
        out[k, :, :N] = d_even
        out[k, :, N : 2 * N] = d_odd
        out[k, :, 2 * N : LEAD] = both
        out[k, :, LEAD:] = merged


def prep_kernel(states, loss, acts, slopes, base):
    base[...] = loss[core()]
    for layer in range(2):
        for i in range(2):
            t = jnp.tanh(states[layer, i].astype(F32))
            acts[layer, i] = rows3(t)
            slopes[layer, i] = H - H * (t * t)


def apply(packed, k, which, e):
    m = one_of_pair(packed[k, :, 2 * N : LEAD], which)
    return e + packed[k, :, which * N : (which + 1) * N].astype(F32) * conv(m, cols3(e))


def upper_kernel(packed, last):
    chips = packed.shape[0]

    def step(r, e):
        k = chips - 1 - r
        x = apply(packed, k, 1, e)
        return apply(packed, k, 0, x) + packed[k, :, LEAD:].astype(F32)

    e = packed[chips - 1, :, LEAD:].astype(F32)
    last[...] = lax.fori_loop(1, chips, step, e).astype(BF16)


def lower_kernel(start, packed, odd, base, mine, other, high, low):
    chips = packed.shape[0]
    spot = lax.rem(lax.axis_index("section") // 2, chips)

    def step(r, e):
        k = chips - 1 - r
        x = apply(packed, k, 1, e)

        @pl.when(k == spot)
        def _():
            high[...] = e
            low[...] = x

        return apply(packed, k, 0, x) + packed[k, :, LEAD:].astype(F32)

    e = lax.fori_loop(0, chips - 1, step, start[...].astype(F32))
    x = apply(packed, 0, 1, e)

    @pl.when(spot == 0)
    def _():
        high[...] = e
        low[...] = x

    at_high = high[...] + base[...]
    at_low = low[...] + odd[...].astype(F32) + base[...]
    even = core() == 0
    mine[...] = jnp.where(even, at_low, at_high)
    other[...] = jnp.where(even, at_high, at_low)


def finish(i, ms, acts, slopes, v, start, starts, sems):
    x3 = cols3(v)
    first = lax.dot_general(x3, acts[1, i], (((1,), (1,)), ((), ())), preferred_element_type=F32)
    v = v + slopes[1, i] * conv(ms[1], x3)
    x3 = cols3(v)
    start[...] = v + slopes[0, i] * conv(ms[0], x3)
    sent = moves([(start, starts.at[0, i])], sems)
    return lax.dot_general(x3, acts[0, i], (((1,), (1,)), ((), ())), preferred_element_type=F32), first, sent


def own_kernel(ms, acts, slopes, mine, sums, starts, start, sems):
    sums[0], sums[1], sent = finish(core(), ms, acts, slopes, mine[...], start, starts, sems)
    settle(sent)


def other_kernel(ms, acts, slopes, other, sums, begun, grads, starts, start, sems):
    del begun
    *products, sent = finish(1 - core(), ms, acts, slopes, other[...], start, starts, sems)
    parts = grads.shape[0]
    rows = C // parts
    g = [(sums[layer] + products[layer]) * H for layer in range(2)]
    cut = 2 * C
    rest = jnp.concatenate([g[0][:, cut:], g[1][:, cut:]], axis=1)
    for d in range(parts):
        pieces = [
            piece[b * C + d * rows : b * C + (d + 1) * rows]
            for piece in (g[0][:, :cut], g[1][:, :cut], rest) for b in range(3)
        ]
        grads[d] = jnp.concatenate(pieces, axis=0).astype(grads.dtype)
    settle(sent)


def total_kernel(parts, out):
    rows = parts.shape[1] // 9
    s = parts[0].astype(F32)
    for d in range(1, parts.shape[0]):
        s = s + parts[d].astype(F32)

    def tap(layer, a, b):
        block, start = (2, layer * C) if a == 2 else (layer, a * C)
        return s[(3 * block + b) * rows : (3 * block + b + 1) * rows, start : start + C]

    for layer in range(2):
        wide = jnp.concatenate([tap(layer, a, b) for a in range(3) for b in range(3)], axis=1)
        out[layer : layer + 1, :] = jnp.concatenate([wide[r : r + 1] for r in range(rows)], axis=1)


def call(kernel, outs, where_in, where_out, scratch, n_sems, flops, moved, grant=16 << 20, aliases={}):
    spaces = {"s": pltpu.SMEM, "v": pltpu.VMEM, "h": pltpu.HBM}
    specs = lambda text: [pl.BlockSpec(memory_space=spaces[k]) for k in text]
    out_specs = specs(where_out)
    return pl.pallas_call(
        kernel,
        out_shape=outs,
        in_specs=specs(where_in),
        out_specs=tuple(out_specs) if isinstance(outs, tuple) else out_specs[0],
        scratch_shapes=[pltpu.VMEM(*one) for one in scratch]
        + ([pltpu.SemaphoreType.DMA((n_sems,))] if n_sems else []),
        input_output_aliases=aliases,
        cost_estimate=pl.CostEstimate(flops=flops, bytes_accessed=moved, transcendentals=0),
        compiler_params=pltpu.CompilerParams(vmem_limit_bytes=grant),
    )


def shards(states, weights, guess, loss):
    sections = lax.axis_size("section")
    nb = lax.axis_size("batch")
    half = sections // 2
    chips = half // 2
    shape = jax.ShapeDtypeStruct
    image, image16 = shape((C, N), F32), shape((C, N), BF16)

    swap = [(i, i ^ 1) for i in range(sections)]
    give, ms, u, g, lc = call(
        give_kernel,
        (shape((C, 2 * N + WIDE), BF16), shape((2, 3 * C, 3 * C), BF16), shape((2, C, N), BF16), image, image),
        "hhhh", "vvvvv", [((2, C, 9 * C), BF16), ((2, C, N), BF16), ((C, N), F32), ((C, N), F32)],
        9, 3 * 10**8, 2 * 10**6,
    )(*[pltpu.with_memory_space_constraint(x, pltpu.HBM) for x in (states, weights, guess, loss)])
    got = lax.ppermute(give, "section", swap)
    keep = call(keep_kernel, shape((C, 2 * N), BF16), "vvvv", "v", [], 0, 3 * 10**8, 10**6)(ms, u, g, lc)
    pairs, odd = call(
        merge_kernel, (shape((chips, C, LEAD + N), BF16), image16), "vvv", "vv", [], 0, 10**8, 3 * 10**6,
    )(keep, got, ms)
    groups = [[x * half + 2 * y + c for y in range(chips)] for x in range(2) for c in range(2)]
    packed = lax.all_to_all(pairs, "section", 0, 0, axis_index_groups=groups, tiled=True)
    acts, slopes, base = call(
        prep_kernel, (shape((2, 2, 3 * C, N), BF16), shape((2, 2, C, N), F32), image),
        "vv", "vvv", [], 0, 10**8, 4 * 10**6,
    )(states, loss)

    last = call(upper_kernel, image16, "v", "v", [], 0, 10**9, 2 * 10**6)(packed)
    carried = lax.ppermute(last, "section", [(i, i - half) for i in range(half, sections)])
    mine, other = call(
        lower_kernel, (image, image), "vvvv", "vv",
        [((C, N), F32), ((C, N), F32)], 0, 12 * 10**8, 2 * 10**6
    )(carried, packed, odd, base)
    theirs = lax.ppermute(other, "section", swap)

    whole = shape((1, 2, C, N), F32)
    sums, starts = call(
        own_kernel, (shape((2, 3 * C, 3 * C), F32), whole), "vvvv", "vh", [((C, N), F32)], 1, 4 * 10**8, 10**6
    )(ms, acts, slopes, mine)
    grads, starts = call(
        other_kernel, (shape((nb, 9 * (C // nb), 2 * C), BF16), whole), "vvvvvh", "vh", [((C, N), F32)], 1,
        4 * 10**8, 10**6, aliases={5: 1},
    )(ms, acts, slopes, theirs, sums, starts)
    grads = lax.all_to_all(grads, "batch", 0, 0, tiled=True)
    total = call(total_kernel, shape((2, 9 * C * C // nb), F32), "v", "v", [], 0, 10**6, 10**6)(grads)
    return starts, total


def solution(mesh):
    placed = (
        P("section", "batch", None, None),
        P("section", None, None),
        P("section", "batch", None, None),
        P("batch", None, None),
    )
    return jax.shard_map(
        shards,
        mesh=mesh,
        in_specs=placed,
        out_specs=(P("section", "batch", None, None), P("section", "batch")),
        check_vma=False,
    )
```

```python
import jax
import jax.numpy as jnp
from jax import lax
from jax.experimental import pallas as pl
from jax.experimental.pallas import tpu as pltpu
from jax.sharding import PartitionSpec as P


H = 0.0625
SIDE = 32
C = 64
N = SIDE * SIDE
LANES = 128
F32 = jnp.float32
BF16 = jnp.bfloat16
WIDE = 640
LEAD = 2 * N + 18 * C


def masked(values, keep):
    return jnp.where(keep, values, jnp.zeros_like(values))


def lane(shape):
    return lax.broadcasted_iota(jnp.int32, shape, len(shape) - 1)


def cols3(v):
    v = v.astype(BF16)
    column = lane(v.shape) & (SIDE - 1)
    ahead = masked(pltpu.roll(v, N - 1, 1), column < SIDE - 1)
    behind = masked(pltpu.roll(v, 1, 1), column > 0)
    return jnp.concatenate([ahead, v, behind], axis=0)


def row_up(t):
    t = pltpu.roll(t, SIDE, 1)
    edge = t[:, :LANES]
    return jnp.concatenate([masked(edge, lane(edge.shape) >= SIDE), t[:, LANES:]], axis=1)


def row_down(t):
    t = pltpu.roll(t, N - SIDE, 1)
    edge = t[:, N - LANES :]
    return jnp.concatenate([t[:, : N - LANES], masked(edge, lane(edge.shape) < LANES - SIDE)], axis=1)


def rows3(t):
    t = t.astype(BF16)
    return jnp.concatenate([row_up(t), t, row_down(t)], axis=0)


def taps(w):
    blocks = [
        jnp.concatenate([w[:, (3 * a + b) * C : (3 * a + b + 1) * C] for a in range(3)], axis=1)
        for b in range(3)
    ]
    return jnp.concatenate(blocks, axis=0).astype(F32).T.astype(BF16)


def conv(m, x3):
    halves = [x3[:, : N // 2], x3[:, N // 2 :]]
    y = jnp.concatenate([jnp.dot(m, half, preferred_element_type=F32) for half in halves], axis=1)
    low = row_down(y[:C].astype(BF16))
    high = row_up(y[2 * C :].astype(BF16))
    return y[C : 2 * C] + low.astype(F32) + high.astype(F32)


def flatten_taps(m):
    wide = [m[a * C : (a + 1) * C, : 2 * C] for a in range(3)]
    thin = [m[a * C : (a + 1) * C, 2 * C :] for a in range(3)]
    return jnp.concatenate(wide + thin, axis=1)


def pair_taps(even, odd):
    thin = [flat[:, (6 + a) * C : (7 + a) * C] for a in range(3) for flat in (even, odd)]
    return jnp.concatenate([even[:, : 6 * C], odd[:, : 6 * C]] + thin, axis=1)


def one_of_pair(pair, which):
    wide = [pair[:, (6 * which + 2 * a) * C : (6 * which + 2 * a + 2) * C] for a in range(3)]
    thin = [pair[:, (12 + 2 * a + which) * C : (13 + 2 * a + which) * C] for a in range(3)]
    return jnp.concatenate([jnp.concatenate(wide, axis=0), jnp.concatenate(thin, axis=0)], axis=1)


def core():
    return lax.rem(lax.axis_index("section"), 2)


def moves(pairs, sems, first=0):
    made = [pltpu.make_async_copy(a, b, sems.at[first + n]) for n, (a, b) in enumerate(pairs)]
    for one in made:
        one.start()
    return made


def settle(made):
    for one in made:
        one.wait()


def part_of(u, g, lc, m0, m1):
    t1 = jnp.tanh(u[1].astype(F32))
    t0 = jnp.tanh(u[0].astype(F32))
    d0 = H - H * (t0 * t0)
    t = (H - H * (t1 * t1)) * conv(m1, cols3(g))
    p = t + d0 * conv(m0, cols3(t - g + 2.0 * lc))
    return (2.0 * d0).astype(BF16), p.astype(BF16)


def give_kernel(states, weights, guess, loss, give, ms, u, g, lc, w, u_give, g_give, lc_give, sems):
    own = core()
    other = 1 - own
    in_w, *first = moves(
        [(weights, w), (states.at[0, other], u_give.at[0]), (states.at[1, other], u_give.at[1]),
         (guess.at[0, other], g_give), (loss.at[other], lc_give)],
        sems,
    )
    second = moves(
        [(states.at[0, own], u.at[0]), (states.at[1, own], u.at[1]), (guess.at[0, own], g), (loss.at[own], lc)],
        sems, 5,
    )
    in_w.wait()
    m1, m0 = taps(w[1]), taps(w[0])
    ms[0], ms[1] = m0, m1
    give[:, 2 * N : 2 * N + 9 * C] = flatten_taps(m0)
    give[:, 2 * N + 9 * C :] = jnp.zeros((C, WIDE - 9 * C), BF16)
    settle(first)
    give[:, :N], give[:, N : 2 * N] = part_of(u_give, g_give[...], lc_give[...], m0, m1)
    settle(second)


def keep_kernel(ms, u, g, lc, keep):
    keep[:, :N], keep[:, N:] = part_of(u, g[...], lc[...], ms[0], ms[1])


def merge_kernel(keep, got, ms, out, odd):
    even = core() == 0
    mine, theirs = flatten_taps(ms[0]), got[:, 2 * N : 2 * N + 9 * C]
    both = pair_taps(jnp.where(even, mine, theirs), jnp.where(even, theirs, mine))
    d_even = jnp.where(even, keep[:, :N], got[:, :N])
    d_odd = jnp.where(even, got[:, :N], keep[:, :N])
    p_even = jnp.where(even, keep[:, N:], got[:, N : 2 * N])
    p_odd = jnp.where(even, got[:, N : 2 * N], keep[:, N:])
    odd[...] = p_odd
    y = conv(one_of_pair(both, 0), cols3(p_odd))
    merged = (p_even.astype(F32) + p_odd.astype(F32) + d_even.astype(F32) * y).astype(BF16)
    for k in range(out.shape[0]):
        out[k, :, :N] = d_even
        out[k, :, N : 2 * N] = d_odd
        out[k, :, 2 * N : LEAD] = both
        out[k, :, LEAD:] = merged


def prep_kernel(states, loss, acts, slopes, base):
    base[...] = loss[core()]
    for layer in range(2):
        for i in range(2):
            t = jnp.tanh(states[layer, i].astype(F32))
            acts[layer, i] = rows3(t)
            slopes[layer, i] = H - H * (t * t)


def apply(packed, k, which, e):
    m = one_of_pair(packed[k, :, 2 * N : LEAD], which)
    return e + packed[k, :, which * N : (which + 1) * N].astype(F32) * conv(m, cols3(e))


def upper_kernel(packed, last):
    chips = packed.shape[0]

    def step(r, e):
        k = chips - 1 - r
        x = apply(packed, k, 1, e)
        return apply(packed, k, 0, x) + packed[k, :, LEAD:].astype(F32)

    e = packed[chips - 1, :, LEAD:].astype(F32)
    last[...] = lax.fori_loop(1, chips, step, e).astype(BF16)


def lower_kernel(start, packed, odd, base, mine, other, high, low):
    chips = packed.shape[0]
    spot = lax.rem(lax.axis_index("section") // 2, chips)

    def step(r, e):
        k = chips - 1 - r
        x = apply(packed, k, 1, e)

        @pl.when(k == spot)
        def _():
            high[...] = e
            low[...] = x

        return apply(packed, k, 0, x) + packed[k, :, LEAD:].astype(F32)

    e = lax.fori_loop(0, chips - 1, step, start[...].astype(F32))
    x = apply(packed, 0, 1, e)

    @pl.when(spot == 0)
    def _():
        high[...] = e
        low[...] = x

    at_high = high[...] + base[...]
    at_low = low[...] + odd[...].astype(F32) + base[...]
    even = core() == 0
    mine[...] = jnp.where(even, at_low, at_high)
    other[...] = jnp.where(even, at_high, at_low)


def finish(i, ms, acts, slopes, v, start):
    x3 = cols3(v)
    first = lax.dot_general(x3, acts[1, i], (((1,), (1,)), ((), ())), preferred_element_type=F32)
    v = v + slopes[1, i] * conv(ms[1], x3)
    x3 = cols3(v)
    start[...] = v + slopes[0, i] * conv(ms[0], x3)
    return lax.dot_general(x3, acts[0, i], (((1,), (1,)), ((), ())), preferred_element_type=F32), first


def own_kernel(ms, acts, slopes, mine, sums, start):
    sums[0], sums[1] = finish(core(), ms, acts, slopes, mine[...], start)


def other_kernel(ms, acts, slopes, other, sums, begun, grads, starts, start, sems):
    sent = moves([(begun, starts.at[0, core()])], sems)
    products = finish(1 - core(), ms, acts, slopes, other[...], start)
    sent += moves([(start, starts.at[0, 1 - core()])], sems, 1)
    parts = grads.shape[0]
    rows = C // parts
    g = [(sums[layer] + products[layer]) * H for layer in range(2)]
    cut = 2 * C
    rest = jnp.concatenate([g[0][:, cut:], g[1][:, cut:]], axis=1)
    for d in range(parts):
        pieces = [
            piece[b * C + d * rows : b * C + (d + 1) * rows]
            for piece in (g[0][:, :cut], g[1][:, :cut], rest) for b in range(3)
        ]
        grads[d] = jnp.concatenate(pieces, axis=0).astype(grads.dtype)
    settle(sent)


def total_kernel(parts, out):
    rows = parts.shape[1] // 9
    s = parts[0].astype(F32)
    for d in range(1, parts.shape[0]):
        s = s + parts[d].astype(F32)

    def tap(layer, a, b):
        block, start = (2, layer * C) if a == 2 else (layer, a * C)
        return s[(3 * block + b) * rows : (3 * block + b + 1) * rows, start : start + C]

    for layer in range(2):
        wide = jnp.concatenate([tap(layer, a, b) for a in range(3) for b in range(3)], axis=1)
        out[layer : layer + 1, :] = jnp.concatenate([wide[r : r + 1] for r in range(rows)], axis=1)


def call(kernel, outs, where_in, where_out, scratch, n_sems, flops, moved, grant=16 << 20):
    spaces = {"s": pltpu.SMEM, "v": pltpu.VMEM, "h": pltpu.HBM}
    specs = lambda text: [pl.BlockSpec(memory_space=spaces[k]) for k in text]
    out_specs = specs(where_out)
    return pl.pallas_call(
        kernel,
        out_shape=outs,
        in_specs=specs(where_in),
        out_specs=tuple(out_specs) if isinstance(outs, tuple) else out_specs[0],
        scratch_shapes=[pltpu.VMEM(*one) for one in scratch]
        + ([pltpu.SemaphoreType.DMA((n_sems,))] if n_sems else []),
        cost_estimate=pl.CostEstimate(flops=flops, bytes_accessed=moved, transcendentals=0),
        compiler_params=pltpu.CompilerParams(vmem_limit_bytes=grant),
    )


def shards(states, weights, guess, loss):
    sections = lax.axis_size("section")
    nb = lax.axis_size("batch")
    half = sections // 2
    chips = half // 2
    shape = jax.ShapeDtypeStruct
    image, image16 = shape((C, N), F32), shape((C, N), BF16)

    swap = [(i, i ^ 1) for i in range(sections)]
    give, ms, u, g, lc = call(
        give_kernel,
        (shape((C, 2 * N + WIDE), BF16), shape((2, 3 * C, 3 * C), BF16), shape((2, C, N), BF16), image, image),
        "hhhh", "vvvvv", [((2, C, 9 * C), BF16), ((2, C, N), BF16), ((C, N), F32), ((C, N), F32)],
        9, 3 * 10**8, 2 * 10**6,
    )(*[pltpu.with_memory_space_constraint(x, pltpu.HBM) for x in (states, weights, guess, loss)])
    got = lax.ppermute(give, "section", swap)
    keep = call(keep_kernel, shape((C, 2 * N), BF16), "vvvv", "v", [], 0, 3 * 10**8, 10**6)(ms, u, g, lc)
    pairs, odd = call(
        merge_kernel, (shape((chips, C, LEAD + N), BF16), image16), "vvv", "vv", [], 0, 10**8, 3 * 10**6,
    )(keep, got, ms)
    groups = [[x * half + 2 * y + c for y in range(chips)] for x in range(2) for c in range(2)]
    packed = lax.all_to_all(pairs, "section", 0, 0, axis_index_groups=groups, tiled=True)
    acts, slopes, base = call(
        prep_kernel, (shape((2, 2, 3 * C, N), BF16), shape((2, 2, C, N), F32), image),
        "vv", "vvv", [], 0, 10**8, 4 * 10**6,
    )(states, loss)

    last = call(upper_kernel, image16, "v", "v", [], 0, 10**9, 2 * 10**6)(packed)
    carried = lax.ppermute(last, "section", [(i, i - half) for i in range(half, sections)])
    mine, other = call(
        lower_kernel, (image, image), "vvvv", "vv",
        [((C, N), F32), ((C, N), F32)], 0, 12 * 10**8, 2 * 10**6
    )(carried, packed, odd, base)
    theirs = lax.ppermute(other, "section", swap)

    sums, begun = call(
        own_kernel, (shape((2, 3 * C, 3 * C), F32), image), "vvvv", "vv", [], 0, 4 * 10**8, 10**6
    )(ms, acts, slopes, mine)
    grads, starts = call(
        other_kernel, (shape((nb, 9 * (C // nb), 2 * C), BF16), shape((1, 2, C, N), F32)), "vvvvvv", "vh",
        [((C, N), F32)], 2, 4 * 10**8, 10**6,
    )(ms, acts, slopes, theirs, sums, begun)
    grads = lax.all_to_all(grads, "batch", 0, 0, tiled=True)
    total = call(total_kernel, shape((2, 9 * C * C // nb), F32), "v", "v", [], 0, 10**6, 10**6)(grads)
    return starts, total


def solution(mesh):
    placed = (
        P("section", "batch", None, None),
        P("section", None, None),
        P("section", "batch", None, None),
        P("batch", None, None),
    )
    return jax.shard_map(
        shards,
        mesh=mesh,
        in_specs=placed,
        out_specs=(P("section", "batch", None, None), P("section", "batch")),
        check_vma=False,
    )
```
